32 devices in a mesh: dp: 8 (over z, x), mp: 4 (over y, core).
Axes of the slice: x: 2, y: 2, z: 4, core: 2. Of those that a mesh axis runs over, the one named last changes fastest.
Arguments:
- rows: float32 [16384, 1280], P(('dp', 'mp')), may hold values from -6 to 6
- lengths: int32 [256], P('dp'), may hold values from 1 to 64, as said below
- freq_class: int32 [256], P(('dp', 'mp')), may hold values from 0 to 2
- freq_table: float32 [3, 1280], replicated, may hold values from -3 to 3
- gain_attn: float32 [1280], replicated, may hold values from 0.5 to 1.5
- gain_mlp: float32 [1280], replicated, may hold values from 0.5 to 1.5
- w_qkv: float32 [3, 1280, 1280], P(None, None, 'mp'), may hold values from -0.15625 to 0.15625
- w_out: float32 [1280, 1280], P('mp'), may hold values from -0.5 to 0.5
- w_gate_up: float32 [2, 1280, 5120], P(None, None, 'mp'), may hold values from -0.15625 to 0.15625
- w_down: float32 [5120, 1280], P('mp'), may hold values from -0.15625 to 0.15625
- cotangent: float32 [16384, 1280], P(('dp', 'mp')), may hold values from -6 to 6
Outputs:
- output: float32 [16384, 1280], P(('dp', 'mp'))
- grad_rows: float32 [16384, 1280], P(('dp', 'mp'))
- grad_qkv: float32 [3, 1280, 1280], P(None, None, 'mp')
- grad_out: float32 [1280, 1280], P('mp')
- grad_gate_up: float32 [2, 1280, 5120], P(None, None, 'mp')
- grad_down: float32 [5120, 1280], P('mp')
- grad_gain_attn: float32 [1280], replicated
- grad_gain_mlp: float32 [1280], replicated
- grad_table: float32 [3, 1280], replicated
The draws below stay inside these ranges and needn't reach their ends.
Inputs may be any that keep to these rules, and one draw needn't show every extreme that they name: `lengths`: the valid patches of a series are the last of its 64 slots; some series has all 64, and some only one.
All inputs are finite; a program needn't handle non-finite values.
Results may differ from the reference program's by a relative error of at most 0.02.
Values may be sent and summed in bfloat16 or wider, within the bound.
A program may use at most 256 MiB of HBM per device.

```python
import jax
import jax.numpy as jnp
from jax import lax

D = 1280
H = 16
HS = 80
FF = 5120
NFREQ = 3
SEQ = 64
SER_GRP = 32
SERIES = 256
TOKENS = 16384


def draw_lengths(key, part):
    groups = SERIES // SER_GRP
    keys_list = jax.random.split(key, 5)
    caps = jax.random.randint(keys_list[0], (groups,), SEQ * 3 // 8, SEQ + 1)
    chosen = jax.random.randint(keys_list[1], (), 0, groups)
    caps = jnp.where(jnp.arange(groups) == chosen, SEQ, caps)
    floors = jnp.maximum(caps // 2, 1)
    spans = caps - floors + 1
    picks = jax.random.randint(keys_list[2], (groups, SER_GRP), 0, 1 << 20)
    series_len = floors[:, None] + picks % spans[:, None]
    longest = jax.random.randint(keys_list[3], (groups,), 0, SER_GRP)
    shortest = (longest + 1 + jax.random.randint(keys_list[4], (groups,), 0, SER_GRP - 1)) % SER_GRP
    slots = jnp.arange(SER_GRP)[None, :]
    series_len = jnp.where(slots == longest[:, None], caps[:, None], series_len)
    series_len = jnp.where(slots == shortest[:, None], 1, series_len)
    return jnp.clip(series_len, 1, SEQ).reshape(SERIES).astype(jnp.int32)


def touch_ends(entries, own_key, smallest, high):
    spot = [jax.random.randint(jax.random.fold_in(own_key, axis), (), 0, length) for axis, length in enumerate(entries.shape)]
    widest = entries.shape.index(max(entries.shape))
    beside = spot[:widest] + [(spot[widest] + 1) % entries.shape[widest]] + spot[widest + 1:]
    return entries.at[tuple(spot)].set(smallest).at[tuple(beside)].set(high)


def block_scale(rng, extent, cuts, smallest, high):
    loudness = 1.0
    for axis_at, blocks in cuts:
        heights = jax.random.uniform(jax.random.fold_in(jax.random.fold_in(rng, 6), axis_at), (blocks,), jnp.float32, smallest / len(cuts), high / len(cuts))
        loudness = loudness * jnp.repeat(jnp.exp(heights), extent[axis_at] // blocks).reshape((-1,) + (1,) * (len(extent) - 1 - axis_at))
    return loudness


def noise(stream_key, shape, spread, bound, cuts=(), kind=jnp.bfloat16):
    entries = spread * jax.random.normal(stream_key, shape, jnp.float32)
    if cuts:
        entries = entries * block_scale(stream_key, shape, cuts, -0.22, 0.18)
    return jnp.clip(entries, -bound, bound).astype(kind)


def setup_inputs(seed: int = 0) -> dict:
    key_of = jax.random.split(jax.random.key(seed), 12)
    return {
        "rows": noise(key_of[0], (TOKENS, D), 1.0, 6.0, ((0, 32),), jnp.float32),
        "lengths": draw_lengths(jax.random.fold_in(key_of[11], 71), 0),
        "freq_class": touch_ends(jax.random.randint(key_of[2], (SERIES,), 0, NFREQ), jax.random.fold_in(key_of[2], 1), 0, NFREQ - 1).astype(jnp.int32),
        "freq_table": noise(key_of[3], (NFREQ, D), 0.5, 3.0, (), jnp.float32),
        "gain_attn": jnp.clip(1.0 + 0.1 * jax.random.normal(key_of[4], (D,), jnp.float32), 0.5, 1.5),
        "gain_mlp": jnp.clip(1.0 + 0.1 * jax.random.normal(key_of[5], (D,), jnp.float32), 0.5, 1.5),
        "w_qkv": noise(key_of[6], (3, D, H * HS), D ** -0.5, 0.15625, ((2, 4),), jnp.float32),
        "w_out": noise(key_of[7], (H * HS, D), (H * HS // 8) ** -0.5, 0.5, ((0, 4),), jnp.float32),
        "w_gate_up": noise(key_of[8], (2, D, FF), D ** -0.5, 0.15625, ((2, 4),), jnp.float32),
        "w_down": noise(key_of[9], (FF, D), (FF // 4) ** -0.5, 0.15625, ((0, 4),), jnp.float32),
        "cotangent": noise(key_of[10], (TOKENS, D), 1.0, 6.0, ((0, 32),), jnp.float32),
    }


@jax.custom_vjp
def low(v):
    return lax.optimization_barrier(v.astype(jnp.bfloat16)).astype(jnp.float32)

@jax.custom_vjp
def low_back(v):
    return v

def low_keep(v):
    return (low(v), None)

def low_pass(kept, grad):
    return (grad,)

def back_keep(v):
    return (v, None)

def back_low(kept, grad):
    return (low(grad),)
low.defvjp(low_keep, low_pass)
low_back.defvjp(back_keep, back_low)
EPSILON = 1e-06
NEGATIVE = -1e+30
HIGHEST = lax.Precision.HIGHEST

def rotate(values, cosines, sines):
    half_width = values.shape[-1] // 2
    first_half = values[..., :half_width]
    second_half = values[..., half_width:]
    return jnp.concatenate([first_half * cosines - second_half * sines, second_half * cosines + first_half * sines], -1)

def series_tables(series_lengths):
    places = jnp.arange(SEQ, dtype=jnp.int32)
    starts = (SEQ - series_lengths).astype(jnp.int32)
    valid_mask = places[None, :] >= starts[:, None]
    positions = (places[None, :] - starts[:, None]).astype(jnp.float32)
    frequency = 10000.0 ** (-2.0 * jnp.arange(HS // 2, dtype=jnp.float32) / HS)
    angles = positions[:, :, None] * frequency[None, None, :]
    return (valid_mask, jnp.cos(angles)[:, :, None, :], jnp.sin(angles)[:, :, None, :])

def allowed_pairs(valid_mask):
    places = jnp.arange(SEQ, dtype=jnp.int32)
    causal = places[:, None] >= places[None, :]
    itself = places[:, None] == places[None, :]
    return causal[None, None] & (valid_mask[:, None, None, :] | itself[None, None])

def forward(rows, freq_table, gain_attn, gain_mlp, w_qkv, w_out, w_gate_up, w_down, onehot, cosines, sines, allowed):
    series_count = allowed.shape[0]
    token_count = rows.shape[0]
    heads_width = w_out.shape[0]
    head_count = heads_width // HS
    start_rows = rows + jnp.dot(onehot, freq_table, precision=HIGHEST)
    normed = low(start_rows * lax.rsqrt(lax.optimization_barrier(jnp.mean(start_rows * start_rows, -1, keepdims=True)) + EPSILON) * gain_attn)
    projected = low_back(jnp.einsum('td,cdf->ctf', normed, low(w_qkv), precision=HIGHEST))
    projected = projected.reshape(3, series_count, SEQ, head_count, HS)
    queries = low(rotate(projected[0], cosines, sines))
    keys = low(rotate(projected[1], cosines, sines))
    values = low(projected[2])
    raw_scores = jnp.einsum('sihe,sjhe->shij', queries, keys, precision=HIGHEST)
    scores = jnp.where(allowed, low_back(raw_scores * HS ** (-0.5)), NEGATIVE)
    attention = jax.nn.softmax(scores, -1)
    mixed = jnp.einsum('shij,sjhe->sihe', low(attention), values, precision=HIGHEST).reshape(token_count, heads_width)
    mixed = low_back(low(mixed))
    after_attn = start_rows + low_back(jnp.dot(mixed, low(w_out), precision=HIGHEST))
    normed_mlp = low(after_attn * lax.rsqrt(lax.optimization_barrier(jnp.mean(after_attn * after_attn, -1, keepdims=True)) + EPSILON) * gain_mlp)
    gate_up = low_back(jnp.einsum('td,cdf->ctf', normed_mlp, low(w_gate_up), precision=HIGHEST))
    hidden = low(jax.nn.silu(gate_up[0]) * gate_up[1])
    return after_attn + low_back(jnp.dot(hidden, low(w_down), precision=HIGHEST))

def reference(rows, lengths, freq_class, freq_table, gain_attn, gain_mlp, w_qkv, w_out, w_gate_up, w_down, cotangent):
    group_count = SERIES // SER_GRP
    group_rows = SER_GRP * SEQ
    params = (freq_table, gain_attn, gain_mlp, w_qkv, w_out, w_gate_up, w_down)

    def one_group(carry, inputs):
        group_x, group_cot, group_lengths, group_class = inputs
        valid_mask, cosines, sines = series_tables(group_lengths)
        allowed = allowed_pairs(valid_mask)
        classes = jnp.repeat(group_class, SEQ)
        onehot = (classes[:, None] == jnp.arange(NFREQ, dtype=jnp.int32)[None, :]).astype(jnp.float32)

        def layer_apply(x_rows, table_arg, gain_one, gain_two, qkv_arg, out_arg, gate_arg, down_arg):
            return forward(x_rows, table_arg, gain_one, gain_two, qkv_arg, out_arg, gate_arg, down_arg, onehot, cosines, sines, allowed)
        result, pullback = jax.vjp(layer_apply, group_x, *params)
        row_mask = valid_mask.reshape(group_rows, 1).astype(jnp.float32)
        grads = pullback(group_cot * row_mask)
        sums, tokens = carry
        sums = tuple((before + update for before, update in zip(sums, grads[1:])))
        tokens = tokens + jnp.sum(row_mask)
        return ((sums, tokens), (result, grads[0]))
    start = (tuple((jnp.zeros_like(weight) for weight in params)), jnp.zeros((), jnp.float32))
    inputs = (rows.reshape(group_count, group_rows, D), cotangent.reshape(group_count, group_rows, D), lengths.reshape(group_count, SER_GRP), freq_class.reshape(group_count, SER_GRP))
    (sums, tokens), (outputs, grad_x) = lax.scan(one_group, start, inputs)
    root_scale = lax.rsqrt(tokens)
    table_sum, gain_one_sum, gain_two_sum, qkv_sum, out_sum, gate_sum, down_sum = sums
    return (outputs.reshape(TOKENS, D), grad_x.reshape(TOKENS, D), qkv_sum * root_scale, out_sum * root_scale, gate_sum * root_scale, down_sum * root_scale, gain_one_sum * root_scale, gain_two_sum * root_scale, table_sum * root_scale)
```

```python
import functools

import jax
import jax.numpy as jnp
import numpy as np
from jax import lax
from jax.experimental import pallas as pl
from jax.experimental.pallas import tpu as pltpu
from jax.sharding import PartitionSpec as P

HS = 80
HALF = HS // 2
LANES = 128
NFREQ = 3
SEQ = 64
PAIR = 128

EPSILON = 1e-06
NEGATIVE = -1e30
HIGHEST = lax.Precision.HIGHEST
LOW = jnp.bfloat16
F32 = jnp.float32
VMEM_LIMIT = 56 * 1024 * 1024
LN2 = float(np.log(2.0))
QSCALE = float(HS**-0.5 / np.log(2.0))


def dot(a, b, ca=1, cb=0):
    return lax.dot_general(a, b, (((ca,), (cb,)), ((), ())), preferred_element_type=F32)


def head_selector(head_count):
    sel = np.zeros((head_count * HS, head_count * LANES), np.float32)
    for h in range(head_count):
        for half in range(2):
            for i in range(HALF):
                sel[h * HS + half * HALF + i, h * LANES + half * (LANES // 2) + i] = 1.0
    return jnp.asarray(sel, LOW)


def slot_tables():
    frequency = 10000.0 ** (-2.0 * np.arange(HALF) / HS)
    angles = np.arange(SEQ)[:, None] * frequency[None, :]
    pad = ((0, 0), (0, LANES // 2 - HALF))
    cosines = np.pad(np.cos(angles), pad)
    sines = np.pad(np.sin(angles), pad)
    return (
        jnp.asarray(np.concatenate([cosines, cosines], 1), F32),
        jnp.asarray(np.concatenate([-sines, sines], 1), F32),
    )


def row_angles(cp, sp, starts, first, count):
    cosines, sines = [], []
    c, s = cp[...], sp[...]
    for i in range(count):
        start = pl.ds(starts[first + i], 1)
        c0, s0 = cp[start, :], sp[start, :]
        cosines.append(c * c0 + s * s0)
        sines.append(s * c0 - c * s0)
    return jnp.concatenate(cosines, 0), jnp.concatenate(sines, 0)


def pair_mask(starts, first):
    j = lax.broadcasted_iota(jnp.int32, (PAIR, PAIR), 0)
    i = lax.broadcasted_iota(jnp.int32, (PAIR, PAIR), 1)
    begin = jnp.where(j < SEQ, starts[first], SEQ + starts[first + 1])
    same = (j < SEQ) == (i < SEQ)
    allowed = (same & (j <= i) & (j >= begin)) | (j == i)
    return jnp.where(allowed, 0.0, NEGATIVE)


def softmax_down(scores):
    exponent = jnp.exp2(scores - jnp.max(scores, 0, keepdims=True))
    return exponent * (1.0 / jnp.sum(exponent, 0, keepdims=True))


def pick(first, xs, a, b):
    @pl.when(first)
    def _():
        xs[...] = a[...]

    @pl.when(jnp.logical_not(first))
    def _():
        xs[...] = b[...]


def put(first, a, b, value):
    @pl.when(first)
    def _():
        a[...] = value

    @pl.when(jnp.logical_not(first))
    def _():
        b[...] = value


def attn_fwd_kernel(nh, starts, x0, x1, wqkv, wout, cp, sp, qkv, mixed, part0, part1, xs):
    step = pl.program_id(0)
    first = step < pl.num_programs(0) // 2
    width = nh * LANES
    rb = xs.shape[0]
    pick(first, xs, x0, x1)
    c, s = row_angles(cp, sp, starts, step * (rb // SEQ), rb // SEQ)
    for part in range(3):
        proj = dot(xs[...], wqkv[part])
        if part == 2:
            qkv[:, 2 * width :] = proj.astype(LOW)
            continue
        scale = QSCALE if part == 0 else 1.0
        cc, ss = c * scale, s * scale
        for h in range(nh):
            p = proj[:, h * LANES : (h + 1) * LANES]
            at = slice(part * width + h * LANES, part * width + (h + 1) * LANES)
            qkv[:, at] = (p * cc + pltpu.roll(p, LANES // 2, 1) * ss).astype(LOW)
    for b in range(rb // PAIR):
        rows = slice(b * PAIR, (b + 1) * PAIR)
        mask = pair_mask(starts, step * (rb // SEQ) + 2 * b)
        get = lambda part, h: qkv[rows, part * width + h * LANES : part * width + (h + 1) * LANES]
        scores = [dot(get(1, h), get(0, h), 1, 1) + mask for h in range(nh)]
        attention = [softmax_down(v).astype(LOW) for v in scores]
        for h in range(nh):
            mixed[rows, h * LANES : (h + 1) * LANES] = dot(attention[h], get(2, h), 0, 0).astype(LOW)
    put(first, part0, part1, dot(mixed[...], wout[...]).astype(LOW))


def attn_bwd_kernel(nh, starts, g0, g1, qkv, wqkv, wout, cp, sp, gproj, part0, part1, gs, gmix):
    step = pl.program_id(0)
    first = step < pl.num_programs(0) // 2
    width = nh * LANES
    rb = gs.shape[0]
    pick(first, gs, g0, g1)
    gmix[...] = dot(gs[...], wout[...], 1, 1).astype(LOW)
    c, s = row_angles(cp, sp, starts, step * (rb // SEQ), rb // SEQ)
    qc, qs = c * HS ** (-0.5), s * HS ** (-0.5)
    kc, ks = c * LN2, s * LN2
    for b in range(rb // PAIR):
        rows = slice(b * PAIR, (b + 1) * PAIR)
        mask = pair_mask(starts, step * (rb // SEQ) + 2 * b)
        at = lambda part, h: slice(part * width + h * LANES, part * width + (h + 1) * LANES)
        heads = range(nh)
        gm = [gmix[rows, at(0, h)] for h in heads]
        scores = [dot(qkv[rows, at(1, h)], qkv[rows, at(0, h)], 1, 1) + mask for h in heads]
        grads = [dot(qkv[rows, at(2, h)], gm[h], 1, 1) for h in heads]
        attention = [softmax_down(v) for v in scores]
        for h in heads:
            gproj[rows, at(2, h)] = dot(attention[h].astype(LOW), gm[h]).astype(LOW)
        low = []
        for h in heads:
            both = attention[h] * grads[h]
            low.append((both - attention[h] * jnp.sum(both, 0, keepdims=True)).astype(LOW))
        for h in heads:
            gk = dot(low[h], qkv[rows, at(0, h)])
            gproj[rows, at(1, h)] = (gk * kc[rows] - pltpu.roll(gk, LANES // 2, 1) * ks[rows]).astype(LOW)
        for h in heads:
            gq = dot(low[h], qkv[rows, at(1, h)], 0, 0)
            gproj[rows, at(0, h)] = (gq * qc[rows] - pltpu.roll(gq, LANES // 2, 1) * qs[rows]).astype(LOW)
    value = dot(gproj[:, :width], wqkv[0], 1, 1)
    value += dot(gproj[:, width : 2 * width], wqkv[1], 1, 1)
    value += dot(gproj[:, 2 * width :], wqkv[2], 1, 1)
    put(first, part0, part1, value.astype(LOW))


def mlp_kernel(x0, x1, y0, y1, wgate, wup, wdown, hidden, gpre, down0, down1, back0, back1, xs, ys):
    first = pl.program_id(0) < pl.num_programs(0) // 2
    pick(first, xs, x0, x1)
    pick(first, ys, y0, y1)
    gate = dot(xs[...], wgate[...])
    sig = jax.nn.sigmoid(gate)
    act = gate * sig
    slope = sig * (1.0 + gate * (1.0 - sig))
    up = dot(xs[...], wup[...])
    hidden[...] = (act * up).astype(LOW)
    gh = dot(ys[...], wdown[...], 1, 1)
    gpre[0] = (gh * up * slope).astype(LOW)
    gpre[1] = (gh * act).astype(LOW)
    put(first, down0, down1, dot(hidden[...], wdown[...]).astype(LOW))
    put(first, back0, back1, (dot(gpre[0], wgate[...], 1, 1) + dot(gpre[1], wup[...], 1, 1)).astype(LOW))


def resident(shape):
    return pl.BlockSpec(shape, lambda i, *_: (0,) * len(shape), pipeline_mode=pl.Buffered(1))


def by_rows(rows, width):
    return pl.BlockSpec((rows, width), lambda i, *_: (i, 0))


def two_parts(rows, width, n):
    return [
        pl.BlockSpec((rows, width), lambda i, *_: (jnp.minimum(i, n - 1), 0)),
        pl.BlockSpec((rows, width), lambda i, *_: (jnp.maximum(i - n, 0), 0)),
    ]


def params():
    return pltpu.CompilerParams(vmem_limit_bytes=VMEM_LIMIT, dimension_semantics=("arbitrary",))


def attn_forward(x, wqkv, wout, starts, tables):
    r, d = x[0].shape
    m = 2 * r
    width = wout.shape[0]
    nh = width // LANES
    rb = min(256, r)
    n = r // rb
    return pl.pallas_call(
        functools.partial(attn_fwd_kernel, nh),
        out_shape=[
            jax.ShapeDtypeStruct((m, 3 * width), LOW),
            jax.ShapeDtypeStruct((m, width), LOW),
            jax.ShapeDtypeStruct((r, d), LOW),
            jax.ShapeDtypeStruct((r, d), LOW),
        ],
        grid_spec=pltpu.PrefetchScalarGridSpec(
            num_scalar_prefetch=1,
            grid=(2 * n,),
            in_specs=[
                *two_parts(rb, d, n),
                resident((3, d, width)),
                resident((width, d)),
                resident((SEQ, LANES)),
                resident((SEQ, LANES)),
            ],
            out_specs=[by_rows(rb, 3 * width), by_rows(rb, width), *two_parts(rb, d, n)],
            scratch_shapes=[pltpu.VMEM((rb, d), LOW)],
        ),
        compiler_params=params(),
        cost_estimate=pl.CostEstimate(
            flops=2 * m * d * 4 * width + 4 * m * PAIR * width,
            bytes_accessed=2 * (2 * m * d + 4 * m * width + 4 * d * width),
            transcendentals=m * PAIR * nh,
        ),
        name="attn_fwd",
    )(starts, *x, wqkv, wout, *tables)


def attn_backward(g, qkv, wqkv, wout, starts, tables):
    r, d = g[0].shape
    m = 2 * r
    width = wout.shape[0]
    nh = width // LANES
    rb = min(256, r)
    n = r // rb
    return pl.pallas_call(
        functools.partial(attn_bwd_kernel, nh),
        out_shape=[
            jax.ShapeDtypeStruct((m, 3 * width), LOW),
            jax.ShapeDtypeStruct((r, d), LOW),
            jax.ShapeDtypeStruct((r, d), LOW),
        ],
        grid_spec=pltpu.PrefetchScalarGridSpec(
            num_scalar_prefetch=1,
            grid=(2 * n,),
            in_specs=[
                *two_parts(rb, d, n),
                by_rows(rb, 3 * width),
                resident((3, d, width)),
                resident((width, d)),
                resident((SEQ, LANES)),
                resident((SEQ, LANES)),
            ],
            out_specs=[by_rows(rb, 3 * width), *two_parts(rb, d, n)],
            scratch_shapes=[pltpu.VMEM((rb, d), LOW), pltpu.VMEM((rb, width), LOW)],
        ),
        compiler_params=params(),
        cost_estimate=pl.CostEstimate(
            flops=2 * m * d * 4 * width + 12 * m * PAIR * width,
            bytes_accessed=2 * (2 * m * d + 6 * m * width + 4 * d * width),
            transcendentals=m * PAIR * nh,
        ),
        name="attn_bwd",
    )(starts, *g, qkv, wqkv, wout, *tables)


def mlp_both(x, gy, wgate, wup, wdown):
    r, d = x[0].shape
    m = 2 * r
    ff = wgate.shape[1]
    rb = min(256, r)
    n = r // rb
    part = jax.ShapeDtypeStruct((r, d), LOW)
    return pl.pallas_call(
        mlp_kernel,
        grid=(2 * n,),
        out_shape=[
            jax.ShapeDtypeStruct((m, ff), LOW),
            jax.ShapeDtypeStruct((2, m, ff), LOW),
            part,
            part,
            part,
            part,
        ],
        in_specs=[
            *two_parts(rb, d, n),
            *two_parts(rb, d, n),
            resident((d, ff)),
            resident((d, ff)),
            resident((ff, d)),
        ],
        out_specs=[
            by_rows(rb, ff),
            pl.BlockSpec((2, rb, ff), lambda i: (0, i, 0)),
            *two_parts(rb, d, n),
            *two_parts(rb, d, n),
        ],
        scratch_shapes=[pltpu.VMEM((rb, d), LOW), pltpu.VMEM((rb, d), LOW)],
        compiler_params=params(),
        cost_estimate=pl.CostEstimate(
            flops=2 * m * d * 6 * ff,
            bytes_accessed=2 * (4 * m * d + 3 * m * ff + 3 * d * ff),
            transcendentals=m * ff,
        ),
        name="mlp_both",
    )(*x, *gy, wgate, wup, wdown)


def weight_grad(a, b, plane=None):
    ra, wide = a[0].shape
    rb, n = b[0].shape[-2:]
    r = min(ra, rb)
    nb = 256 if n % 256 == 0 else 128
    if plane is None:
        b_spec = pl.BlockSpec((rb, nb), lambda i: (0, i))
    else:
        b_spec = pl.BlockSpec((None, rb, nb), lambda i: (plane, 0, i))

    def kernel(*refs):
        xs, ys, out = refs[: len(a)], refs[len(a) : -1], refs[-1]
        total = None
        for at in range(0, len(a) * ra, r):
            x = xs[at // ra][at % ra : at % ra + r]
            y = ys[at // rb][at % rb : at % rb + r]
            part = dot(x, y, 0, 0)
            total = part if total is None else total + part
        out[...] = total.astype(LOW)

    return pl.pallas_call(
        kernel,
        grid=(n // nb,),
        out_shape=jax.ShapeDtypeStruct((wide, n), LOW),
        in_specs=[resident((ra, wide))] * len(a) + [b_spec] * len(b),
        out_specs=pl.BlockSpec((wide, nb), lambda i: (0, i)),
        compiler_params=params(),
        cost_estimate=pl.CostEstimate(
            flops=2 * len(a) * ra * wide * n,
            bytes_accessed=2 * (len(a) * ra * (wide + n) + wide * n),
            transcendentals=0,
        ),
        name="weight_grad",
    )(*a, *b)


def attn_weight_grad(gproj, mixed, normed, ga, selector):
    m, wide = gproj[0].shape
    width = wide // 3
    r, d = normed[0].shape
    real = selector.shape[0]
    chunks = len(normed)
    kb = 256 if d % 256 == 0 else d

    def kernel(*refs):
        gp, mx = refs[: len(gproj)], refs[len(gproj) : 2 * len(gproj)]
        nm, g, sel, out = refs[2 * len(gproj) : -2 - chunks], refs[-2 - chunks : -2], refs[-2], refs[-1]
        for c in range(4):
            total = None
            for i in range(chunks):
                k, at = i * r // m, i * r % m
                x = mx[k][at : at + r] if c == 3 else gp[k][at : at + r, c * width : (c + 1) * width]
                part = dot(x, (g if c == 3 else nm)[i][...], 0, 0)
                total = part if total is None else total + part
            out[c * real : (c + 1) * real] = dot(sel[...], total.astype(LOW)).astype(LOW)

    return pl.pallas_call(
        kernel,
        grid=(d // kb,),
        out_shape=jax.ShapeDtypeStruct((4 * real, d), LOW),
        in_specs=[resident((m, wide))] * len(gproj)
        + [resident((m, width))] * len(mixed)
        + [pl.BlockSpec((r, kb), lambda i: (0, i))] * (2 * chunks)
        + [resident((real, width))],
        out_specs=pl.BlockSpec((4 * real, kb), lambda i: (0, i)),
        compiler_params=params(),
        cost_estimate=pl.CostEstimate(
            flops=2 * chunks * r * d * 4 * width,
            bytes_accessed=2 * chunks * r * (4 * width + 2 * d),
            transcendentals=0,
        ),
        name="attn_weight_grad",
    )(*gproj, *mixed, *normed, *ga, selector)


class Group:
    def __init__(self, mesh):
        self.n = mesh.shape["mp"]
        self.chips = self.n // 2

    def core(self, x):
        return lax.ppermute(x, "mp", [(i, i ^ 1) for i in range(self.n)])

    def from_chip(self, x, k):
        return lax.ppermute(x, "mp", [((i + 2 * k) % self.n, i) for i in range(self.n)])

    def to_chip(self, x, k):
        return lax.ppermute(x, "mp", [(i, (i + 2 * k) % self.n) for i in range(self.n)])

    def gather(self, x):
        mine = [x] + [self.from_chip(x, k) for k in range(1, self.chips)]
        return [(v, self.core(v)) for v in mine]

    def scatter(self, parts):
        total = None
        for k in reversed(range(self.chips)):
            mine = parts[k][0].astype(F32) + self.core(parts[k][1]).astype(F32)
            if k:
                mine = self.to_chip(mine.astype(LOW), k).astype(F32)
            total = mine if total is None else total + mine
        return total


OUTER = 4
CHUNK = 80
MESH = pl.DeviceIdType.MESH


def sum_kernel(inner, group, early, halves, late_pieces, *refs):
    count = len(halves)
    full, refs = refs[:count], refs[count:]
    got, refs = refs[:early], refs[early:]
    small, out, small_out, refs = *refs[:3], refs[3:]
    loc, rc, rb1, rb2, tot, refs = *refs[:5], refs[5:]
    load, late_send, late_recv, s1, r1, s2, r2, s3, r3, s4, r4, keep, refs = *refs[:12], refs[12:]
    sm0, sm1, sm2, small_send, small_recv = refs
    dp = lax.axis_index("dp")
    mp = lax.axis_index("mp")
    place, side = dp // inner, lax.rem(dp, inner)
    outside = jnp.logical_or(place == 0, place == OUTER - 1)
    inside = jnp.logical_not(outside)
    beside = jnp.where(place < OUTER // 2, 1 - place, 5 - place)
    across = (OUTER - 1) - place
    peers = [lax.rem(side + j, inner) for j in range(1, inner)]
    at = lambda p, i: (p * inner + i, mp)

    rounds = []
    me = (mp, side, place)
    others = [
        [(dp, lax.rem(mp + j, group)) for j in range(1, group)],
        [at(place, peer) for peer in peers],
        [at(lax.rem(place + j, OUTER), side) for j in range(1, OUTER)],
    ]
    used = 0
    for mine, buf, devices in zip(me, (sm0, sm1, sm2), others):
        copies = []
        for device in devices:
            copies.append(
                pltpu.make_async_remote_copy(
                    src_ref=buf.at[mine], dst_ref=buf.at[mine], send_sem=small_send.at[used],
                    recv_sem=small_recv.at[used], device_id=device, device_id_type=MESH,
                )
            )
            used += 1
        rounds.append((mine, buf, copies))

    def small_round(i):
        if i:
            for copy in rounds[i - 1][2]:
                copy.wait()
            buf = rounds[i - 1][1]
            value = buf[0]
            for j in range(1, buf.shape[0]):
                value += buf[j]
        else:
            value = small[...]
        if i < len(rounds):
            mine, buf, copies = rounds[i]
            buf[mine] = value
            for copy in copies:
                copy.start()
        else:
            small_out[...] = value

    barrier = pltpu.get_barrier_semaphore()
    for devices in others:
        for device in devices:
            pl.semaphore_signal(barrier, inc=1, device_id=device, device_id_type=MESH)
    pl.semaphore_wait(barrier, sum(len(devices) for devices in others))

    offsets = [sum(halves[:p]) for p in range(count)]
    chunks = sum(halves) // CHUNK

    late = count - 1
    late_copies = []
    for j, peer in enumerate(peers):
        for c in range(late_pieces):
            rows = halves[late] // late_pieces
            late_copies.append(
                pltpu.make_async_remote_copy(
                    src_ref=full[late].at[pl.ds(peer * halves[late] + c * rows, rows)],
                    dst_ref=rc.at[j, pl.ds(offsets[late] + c * rows, rows)],
                    send_sem=late_send.at[j * late_pieces + c],
                    recv_sem=late_recv.at[j * late_pieces + c],
                    device_id=at(place, peer),
                    device_id_type=MESH,
                )
            )
    for copy in late_copies:
        copy.start()

    loads = []
    for p in range(count):
        one = [(full[p].at[pl.ds(side * halves[p], halves[p])], loc.at[pl.ds(offsets[p], halves[p])])]
        if p < early:
            for j in range(inner - 1):
                one.append((got[p].at[j], rc.at[j, pl.ds(offsets[p], halves[p])]))
        loads.append(
            [pltpu.make_async_copy(a, b, load.at[p * inner + i]) for i, (a, b) in enumerate(one)]
        )
    for one in loads:
        for copy in one:
            copy.start()
    small_round(0)

    def to_beside(src, dst, send, recv, t):
        rows = pl.ds(t * CHUNK, CHUNK)
        return pltpu.make_async_remote_copy(
            src_ref=src.at[rows], dst_ref=dst.at[rows], send_sem=send.at[t], recv_sem=recv.at[t],
            device_id=at(beside, side), device_id_type=MESH,
        )

    def to_across(t):
        rows = pl.ds(t * CHUNK, CHUNK)
        return pltpu.make_async_remote_copy(
            src_ref=loc.at[rows], dst_ref=rb2.at[rows], send_sem=s2.at[t], recv_sem=r2.at[t],
            device_id=at(across, side), device_id_type=MESH,
        )

    def to_peer(j, t):
        rows = pl.ds(t * CHUNK, CHUNK)
        return pltpu.make_async_remote_copy(
            src_ref=tot.at[rows], dst_ref=out.at[side, rows], send_sem=s4.at[j, t], recv_sem=r4.at[j, t],
            device_id=at(place, peers[j]), device_id_type=MESH,
        )

    def to_self(t):
        rows = pl.ds(t * CHUNK, CHUNK)
        return pltpu.make_async_copy(tot.at[rows], out.at[side, rows], keep.at[t])

    def hand_out(t):
        for j in range(inner - 1):
            to_peer(j, t).start()
        to_self(t).start()

    def step(t, carry):
        rows = pl.ds(pl.multiple_of(t * CHUNK, CHUNK), CHUNK)

        for i in range(1, len(rounds) + 1):

            @pl.when(t == 2 * i)
            def _(i=i):
                small_round(i)

        @pl.when(t < chunks)
        def _():
            for p in range(count):

                @pl.when(t == offsets[p] // CHUNK)
                def _(p=p):
                    for copy in loads[p]:
                        copy.wait()

            for c in range(late_pieces):

                @pl.when(t == (offsets[late] + c * (halves[late] // late_pieces)) // CHUNK)
                def _(c=c):
                    for j in range(inner - 1):
                        late_copies[j * late_pieces + c].wait_recv()

            total = loc[rows].astype(F32)
            for j in range(inner - 1):
                total += rc[j, rows].astype(F32)
            loc[rows] = total.astype(LOW)

            @pl.when(outside)
            def _():
                to_beside(loc, rb1, s1, r1, t).start()

            @pl.when(inside)
            def _():
                to_beside(loc, rb1, s1, r1, t).wait_recv()
                loc[rows] = (loc[rows].astype(F32) + rb1[rows].astype(F32)).astype(LOW)
                to_across(t).start()

        u = t - 1

        @pl.when(jnp.logical_and(inside, jnp.logical_and(u >= 0, u < chunks)))
        def _():
            ready = pl.ds(pl.multiple_of(u * CHUNK, CHUNK), CHUNK)
            to_across(u).wait_recv()
            tot[ready] = (loc[ready].astype(F32) + rb2[ready].astype(F32)).astype(LOW)
            to_beside(tot, tot, s3, r3, u).start()
            hand_out(u)

        w = t - LAG

        @pl.when(jnp.logical_and(outside, w >= 0))
        def _():
            to_beside(tot, tot, s3, r3, w).wait_recv()
            hand_out(w)

        return carry

    lax.fori_loop(0, chunks + LAG, step, 0)

    def finish(t, carry):
        @pl.when(outside)
        def _():
            to_beside(loc, rb1, s1, r1, t).wait_send()

        @pl.when(inside)
        def _():
            to_across(t).wait_send()
            to_beside(tot, tot, s3, r3, t).wait_send()

        for j in range(inner - 1):
            to_peer(j, t).wait()
        to_self(t).wait()
        return carry

    lax.fori_loop(0, chunks, finish, 0)
    for copy in late_copies:
        copy.wait_send()


LAG = 6


class Reducer:
    def __init__(self, mesh):
        self.inner = mesh.shape["dp"] // OUTER
        self.group = mesh.shape["mp"]

    def exchange(self, x):
        side = lax.rem(lax.axis_index("dp"), self.inner)
        rows = x.shape[0] // self.inner
        got = []
        for j in range(1, self.inner):
            pairs = []
            for o in range(OUTER):
                for i in range(self.inner):
                    pairs.append((o * self.inner + i, o * self.inner + (i + j) % self.inner))
            share = lax.dynamic_slice_in_dim(x, lax.rem(side + j, self.inner) * rows, rows)
            got.append(lax.ppermute(share, "dp", pairs))
        return jnp.stack(got)

    def reduce(self, pieces, got, small):
        inner = self.inner
        width = pieces[0].shape[1]
        halves = tuple(p.shape[0] // inner for p in pieces)
        share = sum(halves)
        chunks = share // CHUNK
        any_spec = pl.BlockSpec(memory_space=pl.ANY)
        late_pieces = halves[-1] // CHUNK // 2
        buffer = pltpu.VMEM((share, width), LOW)
        sems = lambda *shape: pltpu.SemaphoreType.DMA(shape)
        return pl.pallas_call(
            functools.partial(sum_kernel, inner, self.group, len(got), halves, late_pieces),
            out_shape=[
                jax.ShapeDtypeStruct((inner, share, width), LOW),
                jax.ShapeDtypeStruct(small.shape, F32),
            ],
            in_specs=[any_spec] * (len(pieces) + len(got)) + [pl.BlockSpec(memory_space=pltpu.VMEM)],
            out_specs=[any_spec, pl.BlockSpec(memory_space=pltpu.VMEM)],
            scratch_shapes=[
                buffer,
                pltpu.VMEM((inner - 1, share, width), LOW),
                buffer,
                buffer,
                buffer,
                sems(len(pieces) * inner),
                sems((inner - 1) * late_pieces),
                sems((inner - 1) * late_pieces),
                *[sems(chunks) for _ in range(6)],
                sems(inner - 1, chunks),
                sems(inner - 1, chunks),
                sems(chunks),
                pltpu.VMEM((self.group, *small.shape), F32),
                pltpu.VMEM((inner, *small.shape), F32),
                pltpu.VMEM((OUTER, *small.shape), F32),
                sems(self.group + inner + OUTER - 3),
                sems(self.group + inner + OUTER - 3),
            ],
            compiler_params=pltpu.CompilerParams(
                collective_id=0, has_side_effects=True, vmem_limit_bytes=VMEM_LIMIT
            ),
            cost_estimate=pl.CostEstimate(flops=0, bytes_accessed=600_000_000, transcendentals=0),
            name="sum_over_dp",
        )(*pieces, *got, small)


def norm_forward(values, gain):
    inverse = lax.rsqrt(jnp.mean(values * values, -1, keepdims=True) + EPSILON)
    return ((values * inverse * gain).astype(LOW), inverse)


def norm_backward(values, inverse, gain, grad_normed):
    normal = values * inverse
    grad_gain = jnp.sum(grad_normed * normal, 0)
    scaled = grad_normed * gain
    grad_values = inverse * (scaled - normal * jnp.mean(scaled * normal, -1, keepdims=True))
    return (grad_values, grad_gain)


def body(
    mesh,
    rows,
    lengths,
    freq_class,
    freq_table,
    gain_attn,
    gain_mlp,
    w_qkv,
    w_out,
    w_gate_up,
    w_down,
    cotangent,
):
    group = Group(mesh)
    reducer = Reducer(mesh)
    local_rows, d = rows.shape
    own_series = local_rows // SEQ
    mp_index = lax.axis_index("mp")
    heads_width = w_out.shape[0]
    head_count = heads_width // HS
    ff = w_down.shape[0]
    chips = range(group.chips)

    places = jnp.arange(group.n, dtype=jnp.int32)
    owners = ((mp_index // 2 + places // 2) % group.chips) * 2 + (mp_index % 2 + places) % 2
    starts = (SEQ - lengths.reshape(group.n, own_series))[owners]
    group_starts = [starts[2 * k : 2 * k + 2].reshape(-1) for k in chips]
    tables = slot_tables()
    slots = jnp.arange(SEQ, dtype=jnp.int32)
    mine_valid = (slots[None, :] >= starts[0][:, None]).astype(F32)

    by_series = lambda v: v.reshape(own_series, SEQ, d)
    picked = freq_table[NFREQ - 1][None]
    for f in range(NFREQ - 1):
        picked = jnp.where((freq_class == f)[:, None], freq_table[f][None], picked)
    start_rows = (by_series(rows) + picked[:, None]).reshape(local_rows, d)
    normed_mine, inverse_attn = norm_forward(start_rows, gain_attn)
    normed = group.gather(normed_mine)
    grad_output = (by_series(cotangent) * mine_valid[:, :, None]).reshape(local_rows, d)
    grad_down_in = group.gather(grad_output.astype(LOW))

    selector = head_selector(head_count)
    qkv_low = jnp.einsum("cdf,fg->cdg", w_qkv.astype(LOW), selector, preferred_element_type=F32).astype(LOW)
    out_low = dot(selector, w_out.astype(LOW), 0, 0).astype(LOW)
    gate_low = w_gate_up[0].astype(LOW)
    up_low = w_gate_up[1].astype(LOW)
    down_low = w_down.astype(LOW)

    fwd = [attn_forward(normed[k], qkv_low, out_low, group_starts[k], tables) for k in chips]
    after_attn = start_rows + group.scatter([f[2:] for f in fwd])
    normed_mlp_mine, inverse_mlp = norm_forward(after_attn, gain_mlp)
    normed_mlp = group.gather(normed_mlp_mine)

    mlp = [mlp_both(normed_mlp[k], grad_down_in[k], gate_low, up_low, down_low) for k in chips]
    grad_normed_mlp = group.scatter([m[4:] for m in mlp])
    output = after_attn + group.scatter([m[2:4] for m in mlp])
    flat = lambda pairs: [v for pair in pairs for v in pair]
    grad_down = weight_grad([m[0] for m in mlp], flat(grad_down_in))
    ups = [weight_grad(flat(normed_mlp), [m[1] for m in mlp], c) for c in range(2)]
    pieces = [grad_down] + (ups if ff >= d else [jnp.concatenate(ups, 1)])
    got = [reducer.exchange(p) for p in pieces]

    grad_rows_mlp, grad_gain_mlp = norm_backward(after_attn, inverse_mlp, gain_mlp, grad_normed_mlp)
    grad_after = grad_output + grad_rows_mlp
    grad_attn_in = group.gather(grad_after.astype(LOW))

    bwd = [
        attn_backward(grad_attn_in[k], fwd[k][0], qkv_low, out_low, group_starts[k], tables) for k in chips
    ]
    grad_normed = group.scatter([b[1:] for b in bwd])
    pieces.append(
        attn_weight_grad(
            [b[0] for b in bwd], [f[1] for f in fwd], flat(normed), flat(grad_attn_in), selector
        )
    )

    grad_rows_attn, grad_gain_attn = norm_backward(start_rows, inverse_attn, gain_attn, grad_normed)
    grad_rows = grad_after + grad_rows_attn
    series_sums = jnp.sum(by_series(grad_rows), 1)
    grad_table = [jnp.sum(jnp.where((freq_class == f)[:, None], series_sums, 0.0), 0) for f in range(NFREQ)]

    tokens = jnp.full((d,), jnp.sum(mine_valid))
    zero = jnp.zeros((d,), F32)
    small = jnp.stack([grad_gain_attn, grad_gain_mlp, *grad_table, tokens, zero, zero])
    sums, small = reducer.reduce(pieces, got, small)
    root_scale = lax.rsqrt(small[2 + NFREQ, 0])
    small = small * root_scale
    finals, offset = [], 0
    for piece in pieces:
        share = piece.shape[0] // reducer.inner
        finals.append(sums[:, offset : offset + share].reshape(piece.shape))
        offset += share
    down_out = finals[0].astype(F32) * root_scale
    if len(finals) == 3:
        gate_up_out = jnp.stack([finals[1][:, :ff], finals[1][:, ff:]]).astype(F32) * root_scale
    else:
        gate_up_out = jnp.stack(finals[1:3]).astype(F32) * root_scale
    identity = jnp.eye(heads_width, dtype=LOW)
    last = finals[-1]
    qkv_out = jnp.stack(
        [dot(last[c * heads_width : (c + 1) * heads_width], identity, 0, 0) * root_scale for c in range(3)]
    )
    out_out = last[3 * heads_width :].astype(F32) * root_scale
    return (
        output,
        grad_rows,
        qkv_out,
        out_out,
        gate_up_out,
        down_out,
        small[0],
        small[1],
        small[2 : 2 + NFREQ],
    )


def solution(mesh):
    return jax.shard_map(
        functools.partial(body, mesh),
        mesh=mesh,
        in_specs=(
            P(("dp", "mp"), None),
            P("dp"),
            P(("dp", "mp")),
            P(),
            P(),
            P(),
            P(None, None, "mp"),
            P("mp", None),
            P(None, None, "mp"),
            P("mp", None),
            P(("dp", "mp"), None),
        ),
        out_specs=(
            P(("dp", "mp"), None),
            P(("dp", "mp"), None),
            P(None, None, "mp"),
            P("mp", None),
            P(None, None, "mp"),
            P("mp", None),
            P(),
            P(),
            P(),
        ),
        check_vma=False,
    )
```

```python
import functools

import jax
import jax.numpy as jnp
import numpy as np
from jax import lax
from jax.experimental import pallas as pl
from jax.experimental.pallas import tpu as pltpu
from jax.sharding import PartitionSpec as P

HS = 80
HALF = HS // 2
LANES = 128
NFREQ = 3
SEQ = 64
BLOCK = 256
PAIR = 128

EPSILON = 1e-06
NEGATIVE = -1e30
HIGHEST = lax.Precision.HIGHEST
LOW = jnp.bfloat16
F32 = jnp.float32
VMEM_LIMIT = 60 * 1024 * 1024
MESH = pl.DeviceIdType.MESH
LN2 = float(np.log(2.0))
QSCALE = float(HS**-0.5 / np.log(2.0))


def dot(a, b, ca=1, cb=0):
    return lax.dot_general(a, b, (((ca,), (cb,)), ((), ())), preferred_element_type=F32)


def head_selector(head_count):
    sel = np.zeros((head_count * HS, head_count * LANES), np.float32)
    for h in range(head_count):
        for half in range(2):
            for i in range(HALF):
                sel[h * HS + half * HALF + i, h * LANES + half * (LANES // 2) + i] = 1.0
    return jnp.asarray(sel, LOW)


def slot_tables():
    frequency = 10000.0 ** (-2.0 * np.arange(HALF) / HS)
    angles = np.arange(SEQ)[:, None] * frequency[None, :]
    pad = ((0, 0), (0, LANES // 2 - HALF))
    cosines = np.pad(np.cos(angles), pad)
    sines = np.pad(np.sin(angles), pad)
    return (
        jnp.asarray(np.concatenate([cosines, cosines], 1), F32),
        jnp.asarray(np.concatenate([-sines, sines], 1), F32),
    )


def row_angles(cp, sp, starts, first, count):
    cosines, sines = [], []
    c, s = cp[...], sp[...]
    for i in range(count):
        start = pl.ds(starts[first + i], 1)
        c0, s0 = cp[start, :], sp[start, :]
        cosines.append(c * c0 + s * s0)
        sines.append(s * c0 - c * s0)
    return jnp.concatenate(cosines, 0), jnp.concatenate(sines, 0)


def pair_mask(starts, first):
    j = lax.broadcasted_iota(jnp.int32, (PAIR, PAIR), 0)
    i = lax.broadcasted_iota(jnp.int32, (PAIR, PAIR), 1)
    begin = jnp.where(j < SEQ, starts[first], SEQ + starts[first + 1])
    same = (j < SEQ) == (i < SEQ)
    allowed = (same & (j <= i) & (j >= begin)) | (j == i)
    return jnp.where(allowed, 0.0, NEGATIVE)


def softmax_down(scores):
    exponent = jnp.exp2(scores - jnp.max(scores, 0, keepdims=True))
    return exponent * (1.0 / jnp.sum(exponent, 0, keepdims=True))


class Links:
    def __init__(self, chips, blocks, rb):
        self.chips, self.blocks, self.rb = chips, blocks, rb
        self.n = 2 * chips
        self.dp, self.mp = lax.axis_index("dp"), lax.axis_index("mp")
        self.core = (self.dp, self.mp + 1 - 2 * lax.rem(self.mp, 2))

    def further(self, k):
        return (self.dp, lax.rem(self.mp + 2 * k, self.n))

    def nearer(self, k):
        return (self.dp, lax.rem(self.mp + 2 * (self.chips - k), self.n))

    def greet(self):
        barrier = pltpu.get_barrier_semaphore()
        for j in range(1, self.n):
            other = (self.dp, lax.rem(self.mp + j, self.n))
            pl.semaphore_signal(barrier, inc=1, device_id=other, device_id_type=MESH)
        pl.semaphore_wait(barrier, self.n - 1)

    def rows(self, b):
        return pl.ds(b * self.rb, self.rb)

    def each(self, body):
        def one(q, carry):
            body(q // self.blocks, lax.rem(q, self.blocks))
            return carry

        lax.fori_loop(0, self.chips * self.blocks, one, 0)


def remote(src, dst, send, recv, device):
    return pltpu.make_async_remote_copy(
        src_ref=src, dst_ref=dst, send_sem=send, recv_sem=recv, device_id=device, device_id_type=MESH
    )


class Gather:
    def __init__(self, links, x, buf, local, core_send, core_recv, chip_send, chip_recv):
        self.links, self.x, self.buf, self.local = links, x, buf, local
        self.core_send, self.core_recv = core_send, core_recv
        self.chip_send, self.chip_recv = chip_send, chip_recv

    def own(self, b):
        rows = self.links.rows(b)
        return pltpu.make_async_copy(self.x.at[rows], self.buf.at[0, 0, rows], self.local.at[b])

    def to_chip(self, k, b):
        rows = self.links.rows(b)
        return remote(
            self.x.at[rows], self.buf.at[k, 0, rows], self.chip_send.at[k, b], self.chip_recv.at[k, b],
            self.links.nearer(k),
        )

    def to_core(self, k, b):
        rows = self.links.rows(b)
        return remote(
            self.buf.at[k, 0, rows], self.buf.at[k, 1, rows], self.core_send.at[k, b], self.core_recv.at[k, b],
            self.links.core,
        )

    def own_to_core(self, b):
        rows = self.links.rows(b)
        return remote(
            self.x.at[rows], self.buf.at[0, 1, rows], self.core_send.at[0, b], self.core_recv.at[0, b],
            self.links.core,
        )

    def start_near(self):
        for b in range(self.links.blocks):
            self.own(b).start()
            self.own_to_core(b).start()

    def start_far(self, b):
        for k in range(1, self.links.chips):
            self.to_chip(k, b).start()

    def arrive(self, k, b, second):
        @pl.when(jnp.logical_and(jnp.logical_not(second), k == 0))
        def _():
            self.own(b).wait()

        @pl.when(jnp.logical_and(jnp.logical_not(second), k > 0))
        def _():
            self.to_chip(k, b).wait_recv()
            self.to_core(k, b).start()

        @pl.when(second)
        def _():
            self.to_core(k, b).wait_recv()

    def finish(self):
        def sent(k, b):
            self.to_core(k, b).wait_send()

            @pl.when(k > 0)
            def _():
                self.to_chip(k, b).wait_send()

        self.links.each(sent)

    @staticmethod
    def scratch(chips, blocks):
        return [pltpu.SemaphoreType.DMA((blocks,))] + [pltpu.SemaphoreType.DMA((chips, blocks))] * 4


class Scatter:
    def __init__(self, links, give, keep, got, far, core_send, core_recv, chip_send, chip_recv):
        self.links, self.give, self.keep, self.got, self.far = links, give, keep, got, far
        self.core_send, self.core_recv = core_send, core_recv
        self.chip_send, self.chip_recv = chip_send, chip_recv

    def to_core(self, k, b):
        rows = self.links.rows(b)
        return remote(
            self.give.at[k, rows], self.got.at[k, rows], self.core_send.at[k, b], self.core_recv.at[k, b],
            self.links.core,
        )

    def to_chip(self, k, b):
        rows = self.links.rows(b)
        return remote(
            self.keep.at[k, rows], self.far.at[k, rows], self.chip_send.at[k, b], self.chip_recv.at[k, b],
            self.links.further(k),
        )

    def put(self, k, b, second, value):
        rows = self.links.rows(b)

        @pl.when(jnp.logical_not(second))
        def _():
            self.keep[k, rows] = value.astype(LOW)

        @pl.when(second)
        def _():
            self.give[k, rows] = value.astype(LOW)
            self.to_core(k, b).start()

    def pair_done(self, k, b):
        rows = self.links.rows(b)
        self.to_core(k, b).wait_recv()

        @pl.when(k > 0)
        def _():
            self.keep[k, rows] = (self.keep[k, rows].astype(F32) + self.got[k, rows].astype(F32)).astype(LOW)
            self.to_chip(k, b).start()

    def total(self, b):
        rows = self.links.rows(b)
        value = self.keep[0, rows].astype(F32) + self.got[0, rows].astype(F32)
        for k in range(1, self.links.chips):
            self.to_chip(k, b).wait_recv()
            value += self.far[k, rows].astype(F32)
        return value

    def finish(self):
        def sent(k, b):
            self.to_core(k, b).wait_send()

            @pl.when(k > 0)
            def _():
                self.to_chip(k, b).wait_send()

        self.links.each(sent)

    @staticmethod
    def scratch(chips, blocks, rows, width):
        return [pltpu.VMEM((chips, rows, width), LOW)] * 4 + [pltpu.SemaphoreType.DMA((chips, blocks))] * 4


def run_blocks(links, arrive, compute, scatters):
    def step(i, carry):
        q, second = i // 2, lax.rem(i, 2) == 1
        k, b = q // links.blocks, lax.rem(q, links.blocks)
        arrive(i, k, b, second)
        for scatter, value in zip(scatters, compute(i, k, b, second)):
            scatter.put(k, b, second, value)

        @pl.when(jnp.logical_and(jnp.logical_not(second), q > 0))
        def _():
            for scatter in scatters:
                scatter.pair_done((q - 1) // links.blocks, lax.rem(q - 1, links.blocks))

        return carry

    pairs = links.chips * links.blocks
    lax.fori_loop(0, 2 * pairs, step, 0)
    for scatter in scatters:
        scatter.pair_done(links.chips - 1, links.blocks - 1)


class Store:
    def __init__(self, sems, pairs):
        self.sems, self.pairs = sems, pairs

    def copies(self, i):
        return [pltpu.make_async_copy(a, b, self.sems.at[i, j]) for j, (a, b) in enumerate(self.pairs(i))]

    def start(self, i):
        for copy in self.copies(i):
            copy.start()

    def wait(self, i):
        for copy in self.copies(i):
            copy.wait()


def loader(sems, pairs):
    copies = [pltpu.make_async_copy(a, b, sems.at[i]) for i, (a, b) in enumerate(pairs)]
    for copy in copies:
        copy.start()
    return copies


def row_block(links, i, k, b, second):
    at = (2 * k + second.astype(jnp.int32)) * (links.blocks * links.rb) + b * links.rb
    return pl.multiple_of(at, links.rb)


def attn_fwd_kernel(nh, chips, blocks, rb, x, start, gain, wqkv_any, wout_any, starts, cp, sp, *refs):
    qkv_out, mixed_out, xg_out, after, normed, refs = *refs[:5], refs[5:]
    xg, wqkv, wout, qkv, mixed, begin, load, store_sems, refs = *refs[:8], refs[8:]
    gather_refs, scatter_refs = refs[:5], refs[5:]
    links = Links(chips, blocks, rb)
    loads = loader(load, [(wqkv_any, wqkv), (wout_any, wout), (start, begin)])
    links.greet()
    gather = Gather(links, x, xg, *gather_refs)
    scatter = Scatter(links, *scatter_refs)
    gather.start_near()
    for b in range(blocks):
        gather.start_far(b)
    loads[0].wait()
    loads[1].wait()
    width = nh * LANES
    series = rb // SEQ

    def places(i):
        q, second = i // 2, lax.rem(i, 2) == 1
        k, b = q // blocks, lax.rem(q, blocks)
        return k, b, lax.rem(i, 2), row_block(links, i, k, b, second)

    def pairs(i):
        k, b, s, at = places(i)
        rows = pl.ds(at, rb)
        return [
            (qkv.at[rows], qkv_out.at[rows]),
            (mixed.at[rows], mixed_out.at[rows]),
            (xg.at[k, s, links.rows(b)], xg_out.at[k, s, links.rows(b)]),
        ]

    store = Store(store_sems, pairs)

    def compute(i, k, b, second):
        s = second.astype(jnp.int32)
        at = row_block(links, i, k, b, second)
        rows = pl.ds(at, rb)
        xs = xg[k, s, links.rows(b)]
        first = at // SEQ
        c, sn = row_angles(cp, sp, starts, first, series)
        for part in range(3):
            proj = dot(xs, wqkv[part])
            if part == 2:
                qkv[rows, 2 * width :] = proj.astype(LOW)
                continue
            scale = QSCALE if part == 0 else 1.0
            cc, ss = c * scale, sn * scale
            for h in range(nh):
                p = proj[:, h * LANES : (h + 1) * LANES]
                cols = slice(part * width + h * LANES, part * width + (h + 1) * LANES)
                qkv[rows, cols] = (p * cc + pltpu.roll(p, LANES // 2, 1) * ss).astype(LOW)
        for p in range(rb // PAIR):
            sub = pl.ds(pl.multiple_of(at + p * PAIR, PAIR), PAIR)
            mask = pair_mask(starts, first + 2 * p)
            get = lambda part, h: qkv[sub, part * width + h * LANES : part * width + (h + 1) * LANES]
            scores = [dot(get(1, h), get(0, h), 1, 1) + mask for h in range(nh)]
            attention = [softmax_down(v).astype(LOW) for v in scores]
            for h in range(nh):
                mixed[sub, h * LANES : (h + 1) * LANES] = dot(attention[h], get(2, h), 0, 0).astype(LOW)
        part = dot(mixed[rows], wout[...])
        store.start(i)
        return [part]

    run_blocks(links, lambda i, k, b, second: gather.arrive(k, b, second), compute, [scatter])
    loads[2].wait()

    def last(b, carry):
        rows = pl.ds(pl.multiple_of(b * rb, rb), rb)
        value = begin[rows] + scatter.total(b)
        after[rows] = value
        inverse = lax.rsqrt(jnp.mean(value * value, -1, keepdims=True) + EPSILON)
        normed[rows] = (value * inverse * gain[...]).astype(LOW)
        return carry

    lax.fori_loop(0, blocks, last, 0)
    gather.finish()
    scatter.finish()

    def stored(i, carry):
        store.wait(i)
        return carry

    lax.fori_loop(0, 2 * chips * blocks, stored, 0)


def norm_backward_block(value, gain, grad_normed, before):
    inverse = lax.rsqrt(jnp.mean(value * value, -1, keepdims=True) + EPSILON)
    normal = value * inverse
    scaled = grad_normed * gain
    grad = before + inverse * (scaled - normal * jnp.mean(scaled * normal, -1, keepdims=True))
    return grad, jnp.sum(grad_normed * normal, 0, keepdims=True)


def mlp_kernel(chips, blocks, rb, x, gy, after, grad_in, gain, wgate_any, wup_any, wdown_any, *refs):
    hidden_out, gpre_out, xg_out, yg_out, own_out, far_out, grad_after, low_after, gain_grad, refs = *refs[:9], refs[9:]
    xg, yg, wgate, wup, wdown, hidden, gpre, begin, before, load, store_sems, down_sems, refs = *refs[:12], refs[12:]
    xg_refs, yg_refs, back_refs = refs[:5], refs[5:10], refs[10:18]
    give, keep, got, down_send, down_recv = refs[18:]
    links = Links(chips, blocks, rb)
    loads = loader(load, [(wgate_any, wgate), (wup_any, wup), (wdown_any, wdown), (after, begin), (grad_in, before)])
    links.greet()
    gather = Gather(links, x, xg, *xg_refs)
    second_gather = Gather(links, gy, yg, *yg_refs)
    back = Scatter(links, *back_refs)
    gather.start_near()
    second_gather.start_near()
    for b in range(blocks):
        gather.start_far(b)

    def down_to_core(k, b):
        rows = links.rows(b)
        return remote(
            give.at[k, rows], got.at[k, rows], down_send.at[k, b], down_recv.at[k, b], links.core
        )

    def pairs(i):
        q, second = i // 2, lax.rem(i, 2) == 1
        k, b, s = q // blocks, lax.rem(q, blocks), lax.rem(i, 2)
        rows = pl.ds(row_block(links, i, k, b, second), rb)
        slot = lax.rem(i, 2)
        return [
            (hidden.at[slot], hidden_out.at[rows]),
            (gpre.at[slot, 0], gpre_out.at[0, rows]),
            (gpre.at[slot, 1], gpre_out.at[1, rows]),
            (xg.at[k, s, links.rows(b)], xg_out.at[k, s, links.rows(b)]),
            (yg.at[k, s, links.rows(b)], yg_out.at[k, s, links.rows(b)]),
        ]

    store = Store(store_sems, pairs)
    steps = 2 * chips * blocks

    def arrive(i, k, b, second):
        for j in range(blocks):

            @pl.when(i == min(blocks + j, 2 * blocks - 1))
            def _(j=j):
                second_gather.start_far(j)

        gather.arrive(k, b, second)

        @pl.when(i == 0)
        def _():
            loads[0].wait()
            loads[1].wait()
            loads[2].wait()

    def compute(i, k, b, second):
        s = second.astype(jnp.int32)
        slot = lax.rem(i, 2)

        @pl.when(i >= 2)
        def _():
            store.wait(i - 2)

        xs = xg[k, s, links.rows(b)]
        gate = dot(xs, wgate[...])
        sig = jax.nn.sigmoid(gate)
        act = gate * sig
        slope = sig * (1.0 + gate * (1.0 - sig))
        up = dot(xs, wup[...])
        hidden[slot] = (act * up).astype(LOW)
        second_gather.arrive(k, b, second)
        gh = dot(yg[k, s, links.rows(b)], wdown[...], 1, 1)
        gpre[slot, 0] = (gh * up * slope).astype(LOW)
        gpre[slot, 1] = (gh * act).astype(LOW)
        grad = dot(gpre[slot, 0], wgate[...], 1, 1) + dot(gpre[slot, 1], wup[...], 1, 1)
        down = dot(hidden[slot], wdown[...]).astype(LOW)
        rows = links.rows(b)

        @pl.when(jnp.logical_not(second))
        def _():
            keep[k, rows] = down

        @pl.when(second)
        def _():
            give[k, rows] = down
            down_to_core(k, b).start()

        store.start(i)
        return [grad]

    run_blocks(links, arrive, compute, [back])

    def down_sum(k, b):
        rows = links.rows(b)
        down_to_core(k, b).wait_recv()
        keep[k, rows] = (keep[k, rows].astype(F32) + got[k, rows].astype(F32)).astype(LOW)

    links.each(down_sum)
    outs = [pltpu.make_async_copy(keep.at[0], own_out, down_sems.at[0])]
    for k in range(1, chips):
        outs.append(pltpu.make_async_copy(keep.at[k], far_out.at[k - 1], down_sems.at[k]))
    for copy in outs:
        copy.start()
    loads[3].wait()
    loads[4].wait()
    gain_grad[...] = jnp.zeros_like(gain_grad)

    def last(b, carry):
        rows = pl.ds(pl.multiple_of(b * rb, rb), rb)
        grad, gains = norm_backward_block(begin[rows], gain[...], back.total(b), before[rows])
        grad_after[rows] = grad
        low_after[rows] = grad.astype(LOW)
        gain_grad[0:1] += gains
        return carry

    lax.fori_loop(0, blocks, last, 0)
    gather.finish()
    second_gather.finish()
    back.finish()
    links.each(lambda k, b: down_to_core(k, b).wait_send())
    for copy in outs:
        copy.wait()
    store.wait(steps - 2)
    store.wait(steps - 1)


def attn_bwd_kernel(nh, chips, blocks, rb, x, start, grad_in, gain, qkv_any, wqkv_any, wout_any, starts, cp, sp, *refs):
    gproj_out, xg_out, grad_rows, gain_grad, refs = *refs[:4], refs[4:]
    xg, wqkv, wout, qkv, gproj, gmix, begin, before, load, store_sems, refs = *refs[:10], refs[10:]
    gather_refs, scatter_refs = refs[:5], refs[5:]
    links = Links(chips, blocks, rb)
    loads = loader(
        load, [(wout_any, wout), (qkv_any, qkv), (wqkv_any, wqkv), (start, begin), (grad_in, before)]
    )
    links.greet()
    gather = Gather(links, x, xg, *gather_refs)
    scatter = Scatter(links, *scatter_refs)
    gather.start_near()
    for b in range(blocks):
        gather.start_far(b)
    for copy in loads[:3]:
        copy.wait()
    width = nh * LANES
    series = rb // SEQ

    def pairs(i):
        q, second = i // 2, lax.rem(i, 2) == 1
        k, b, s = q // blocks, lax.rem(q, blocks), lax.rem(i, 2)
        rows = pl.ds(row_block(links, i, k, b, second), rb)
        return [
            (gproj.at[rows], gproj_out.at[rows]),
            (xg.at[k, s, links.rows(b)], xg_out.at[k, s, links.rows(b)]),
        ]

    store = Store(store_sems, pairs)

    def compute(i, k, b, second):
        s = second.astype(jnp.int32)
        at = row_block(links, i, k, b, second)
        rows = pl.ds(at, rb)
        first = at // SEQ
        gmix[...] = dot(xg[k, s, links.rows(b)], wout[...], 1, 1).astype(LOW)
        c, sn = row_angles(cp, sp, starts, first, series)
        qc, qs = c * HS ** (-0.5), sn * HS ** (-0.5)
        kc, ks = c * LN2, sn * LN2
        for p in range(rb // PAIR):
            part = slice(p * PAIR, (p + 1) * PAIR)
            sub = pl.ds(pl.multiple_of(at + p * PAIR, PAIR), PAIR)
            mask = pair_mask(starts, first + 2 * p)
            col = lambda part, h: slice(part * width + h * LANES, part * width + (h + 1) * LANES)
            heads = range(nh)
            gm = [gmix[part, col(0, h)] for h in heads]
            scores = [dot(qkv[sub, col(1, h)], qkv[sub, col(0, h)], 1, 1) + mask for h in heads]
            grads = [dot(qkv[sub, col(2, h)], gm[h], 1, 1) for h in heads]
            attention = [softmax_down(v) for v in scores]
            for h in heads:
                gproj[sub, col(2, h)] = dot(attention[h].astype(LOW), gm[h]).astype(LOW)
            low = []
            for h in heads:
                both = attention[h] * grads[h]
                low.append((both - attention[h] * jnp.sum(both, 0, keepdims=True)).astype(LOW))
            for h in heads:
                g = dot(low[h], qkv[sub, col(0, h)])
                gproj[sub, col(1, h)] = (g * kc[part] - pltpu.roll(g, LANES // 2, 1) * ks[part]).astype(LOW)
            for h in heads:
                g = dot(low[h], qkv[sub, col(1, h)], 0, 0)
                gproj[sub, col(0, h)] = (g * qc[part] - pltpu.roll(g, LANES // 2, 1) * qs[part]).astype(LOW)
        value = dot(gproj[rows, :width], wqkv[0], 1, 1)
        value += dot(gproj[rows, width : 2 * width], wqkv[1], 1, 1)
        value += dot(gproj[rows, 2 * width :], wqkv[2], 1, 1)
        store.start(i)
        return [value]

    run_blocks(links, lambda i, k, b, second: gather.arrive(k, b, second), compute, [scatter])
    loads[3].wait()
    loads[4].wait()
    gain_grad[...] = jnp.zeros_like(gain_grad)

    def last(b, carry):
        rows = pl.ds(pl.multiple_of(b * rb, rb), rb)
        grad, gains = norm_backward_block(begin[rows], gain[...], scatter.total(b), before[rows])
        grad_rows[rows] = grad
        gain_grad[0:1] += gains
        return carry

    lax.fori_loop(0, blocks, last, 0)
    gather.finish()
    scatter.finish()

    def stored(i, carry):
        store.wait(i)
        return carry

    lax.fori_loop(0, 2 * chips * blocks, stored, 0)


def resident(shape):
    return pl.BlockSpec(shape, lambda i, *_: (0,) * len(shape), pipeline_mode=pl.Buffered(1))


def by_rows(rows, width):
    return pl.BlockSpec((rows, width), lambda i, *_: (i, 0))


def params(collective_id=None):
    return pltpu.CompilerParams(
        vmem_limit_bytes=VMEM_LIMIT, collective_id=collective_id, has_side_effects=collective_id is not None
    )


ANY = pl.BlockSpec(memory_space=pl.ANY)
WHOLE = pl.BlockSpec(memory_space=pltpu.VMEM)
SCALARS = pl.BlockSpec(memory_space=pltpu.SMEM)


def sems(*shape):
    return pltpu.SemaphoreType.DMA(shape)


def attn_forward(chips, x, start, gain, wqkv, wout, starts, tables):
    r, d = x.shape
    m = 2 * chips * r
    width = wout.shape[0]
    nh = width // LANES
    rb = min(BLOCK, r)
    blocks = r // rb
    steps = 2 * chips * blocks
    return pl.pallas_call(
        functools.partial(attn_fwd_kernel, nh, chips, blocks, rb),
        out_shape=[
            jax.ShapeDtypeStruct((m, 3 * width), LOW),
            jax.ShapeDtypeStruct((m, width), LOW),
            jax.ShapeDtypeStruct((chips, 2, r, d), LOW),
            jax.ShapeDtypeStruct((r, d), F32),
            jax.ShapeDtypeStruct((r, d), LOW),
        ],
        in_specs=[ANY, ANY, WHOLE, ANY, ANY, SCALARS, WHOLE, WHOLE],
        out_specs=[ANY, ANY, ANY, WHOLE, WHOLE],
        scratch_shapes=[
            pltpu.VMEM((chips, 2, r, d), LOW),
            pltpu.VMEM((3, d, width), LOW),
            pltpu.VMEM((width, d), LOW),
            pltpu.VMEM((m, 3 * width), LOW),
            pltpu.VMEM((m, width), LOW),
            pltpu.VMEM((r, d), F32),
            sems(3),
            sems(steps, 3),
            *Gather.scratch(chips, blocks),
            *Scatter.scratch(chips, blocks, r, d),
        ],
        compiler_params=params(1),
        name="attn_fwd",
    )(x, start, gain, wqkv, wout, starts, *tables)


def mlp_both(chips, x, gy, after, grad_in, gain, wgate, wup, wdown):
    r, d = x.shape
    m = 2 * chips * r
    ff = wgate.shape[1]
    rb = min(BLOCK, r)
    blocks = r // rb
    steps = 2 * chips * blocks
    group = jax.ShapeDtypeStruct((chips, 2, r, d), LOW)
    return pl.pallas_call(
        functools.partial(mlp_kernel, chips, blocks, rb),
        out_shape=[
            jax.ShapeDtypeStruct((m, ff), LOW),
            jax.ShapeDtypeStruct((2, m, ff), LOW),
            group,
            group,
            jax.ShapeDtypeStruct((r, d), LOW),
            jax.ShapeDtypeStruct((chips - 1, r, d), LOW),
            jax.ShapeDtypeStruct((r, d), F32),
            jax.ShapeDtypeStruct((r, d), LOW),
            jax.ShapeDtypeStruct((8, d), F32),
        ],
        in_specs=[ANY, ANY, ANY, ANY, WHOLE, ANY, ANY, ANY],
        out_specs=[ANY] * 6 + [WHOLE] * 3,
        scratch_shapes=[
            pltpu.VMEM((chips, 2, r, d), LOW),
            pltpu.VMEM((chips, 2, r, d), LOW),
            pltpu.VMEM((d, ff), LOW),
            pltpu.VMEM((d, ff), LOW),
            pltpu.VMEM((ff, d), LOW),
            pltpu.VMEM((2, rb, ff), LOW),
            pltpu.VMEM((2, 2, rb, ff), LOW),
            pltpu.VMEM((r, d), F32),
            pltpu.VMEM((r, d), F32),
            sems(5),
            sems(steps, 5),
            sems(chips),
            *Gather.scratch(chips, blocks),
            *Gather.scratch(chips, blocks),
            *Scatter.scratch(chips, blocks, r, d),
            *[pltpu.VMEM((chips, r, d), LOW)] * 3,
            sems(chips, blocks),
            sems(chips, blocks),
        ],
        compiler_params=params(2),
        name="mlp_both",
    )(x, gy, after, grad_in, gain, wgate, wup, wdown)


def attn_backward(chips, x, start, grad_in, gain, qkv, wqkv, wout, starts, tables):
    r, d = x.shape
    m = 2 * chips * r
    width = wout.shape[0]
    nh = width // LANES
    rb = min(BLOCK, r)
    blocks = r // rb
    steps = 2 * chips * blocks
    return pl.pallas_call(
        functools.partial(attn_bwd_kernel, nh, chips, blocks, rb),
        out_shape=[
            jax.ShapeDtypeStruct((m, 3 * width), LOW),
            jax.ShapeDtypeStruct((chips, 2, r, d), LOW),
            jax.ShapeDtypeStruct((r, d), F32),
            jax.ShapeDtypeStruct((8, d), F32),
        ],
        in_specs=[ANY, ANY, ANY, WHOLE, ANY, ANY, ANY, SCALARS, WHOLE, WHOLE],
        out_specs=[ANY, ANY, WHOLE, WHOLE],
        scratch_shapes=[
            pltpu.VMEM((chips, 2, r, d), LOW),
            pltpu.VMEM((3, d, width), LOW),
            pltpu.VMEM((width, d), LOW),
            pltpu.VMEM((m, 3 * width), LOW),
            pltpu.VMEM((m, 3 * width), LOW),
            pltpu.VMEM((rb, width), LOW),
            pltpu.VMEM((r, d), F32),
            pltpu.VMEM((r, d), F32),
            sems(5),
            sems(steps, 2),
            *Gather.scratch(chips, blocks),
            *Scatter.scratch(chips, blocks, r, d),
        ],
        compiler_params=params(3),
        name="attn_bwd",
    )(x, start, grad_in, gain, qkv, wqkv, wout, starts, *tables)


def weight_grad(a, b, plane=None):
    ra, wide = a[0].shape
    rb, n = b[0].shape[-2:]
    r = min(ra, rb)
    nb = 256 if n % 256 == 0 else 128
    if plane is None:
        b_spec = pl.BlockSpec((rb, nb), lambda i: (0, i))
    else:
        b_spec = pl.BlockSpec((None, rb, nb), lambda i: (plane, 0, i))

    def kernel(*refs):
        xs, ys, out = refs[: len(a)], refs[len(a) : -1], refs[-1]
        total = None
        for at in range(0, len(a) * ra, r):
            x = xs[at // ra][at % ra : at % ra + r]
            y = ys[at // rb][at % rb : at % rb + r]
            part = dot(x, y, 0, 0)
            total = part if total is None else total + part
        out[...] = total.astype(LOW)

    return pl.pallas_call(
        kernel,
        grid=(n // nb,),
        out_shape=jax.ShapeDtypeStruct((wide, n), LOW),
        in_specs=[resident((ra, wide))] * len(a) + [b_spec] * len(b),
        out_specs=pl.BlockSpec((wide, nb), lambda i: (0, i)),
        compiler_params=params(),
        cost_estimate=pl.CostEstimate(
            flops=2 * len(a) * ra * wide * n,
            bytes_accessed=2 * (len(a) * ra * (wide + n) + wide * n),
            transcendentals=0,
        ),
        name="weight_grad",
    )(*a, *b)


def attn_weight_grad(gproj, mixed, normed, ga, selector):
    m, wide = gproj[0].shape
    width = wide // 3
    r, d = normed[0].shape
    real = selector.shape[0]
    chunks = len(normed)
    kb = 256 if d % 256 == 0 else d

    def kernel(*refs):
        gp, mx = refs[: len(gproj)], refs[len(gproj) : 2 * len(gproj)]
        nm, g, sel, out = refs[2 * len(gproj) : -2 - chunks], refs[-2 - chunks : -2], refs[-2], refs[-1]
        for c in range(4):
            total = None
            for i in range(chunks):
                k, at = i * r // m, i * r % m
                x = mx[k][at : at + r] if c == 3 else gp[k][at : at + r, c * width : (c + 1) * width]
                part = dot(x, (g if c == 3 else nm)[i][...], 0, 0)
                total = part if total is None else total + part
            out[c * real : (c + 1) * real] = dot(sel[...], total.astype(LOW)).astype(LOW)

    return pl.pallas_call(
        kernel,
        grid=(d // kb,),
        out_shape=jax.ShapeDtypeStruct((4 * real, d), LOW),
        in_specs=[resident((m, wide))] * len(gproj)
        + [resident((m, width))] * len(mixed)
        + [pl.BlockSpec((r, kb), lambda i: (0, i))] * (2 * chunks)
        + [resident((real, width))],
        out_specs=pl.BlockSpec((4 * real, kb), lambda i: (0, i)),
        compiler_params=params(),
        cost_estimate=pl.CostEstimate(
            flops=2 * chunks * r * d * 4 * width,
            bytes_accessed=2 * chunks * r * (4 * width + 2 * d),
            transcendentals=0,
        ),
        name="attn_weight_grad",
    )(*gproj, *mixed, *normed, *ga, selector)


OUTER = 4
CHUNK = 80


def sum_kernel(inner, group, early, halves, late_pieces, *refs):
    count = len(halves)
    full, refs = refs[:count], refs[count:]
    got, refs = refs[:early], refs[early:]
    small, out, small_out, refs = *refs[:3], refs[3:]
    loc, rc, rb1, rb2, tot, refs = *refs[:5], refs[5:]
    load, late_send, late_recv, s1, r1, s2, r2, s3, r3, s4, r4, keep, refs = *refs[:12], refs[12:]
    sm0, sm1, sm2, small_send, small_recv = refs
    dp = lax.axis_index("dp")
    mp = lax.axis_index("mp")
    place, side = dp // inner, lax.rem(dp, inner)
    outside = jnp.logical_or(place == 0, place == OUTER - 1)
    inside = jnp.logical_not(outside)
    beside = jnp.where(place < OUTER // 2, 1 - place, 5 - place)
    across = (OUTER - 1) - place
    peers = [lax.rem(side + j, inner) for j in range(1, inner)]
    at = lambda p, i: (p * inner + i, mp)

    rounds = []
    me = (mp, side, place)
    others = [
        [(dp, lax.rem(mp + j, group)) for j in range(1, group)],
        [at(place, peer) for peer in peers],
        [at(lax.rem(place + j, OUTER), side) for j in range(1, OUTER)],
    ]
    used = 0
    for mine, buf, devices in zip(me, (sm0, sm1, sm2), others):
        copies = []
        for device in devices:
            copies.append(
                pltpu.make_async_remote_copy(
                    src_ref=buf.at[mine], dst_ref=buf.at[mine], send_sem=small_send.at[used],
                    recv_sem=small_recv.at[used], device_id=device, device_id_type=MESH,
                )
            )
            used += 1
        rounds.append((mine, buf, copies))

    def small_round(i):
        if i:
            for copy in rounds[i - 1][2]:
                copy.wait()
            buf = rounds[i - 1][1]
            value = buf[0]
            for j in range(1, buf.shape[0]):
                value += buf[j]
        else:
            value = small[...]
        if i < len(rounds):
            mine, buf, copies = rounds[i]
            buf[mine] = value
            for copy in copies:
                copy.start()
        else:
            small_out[...] = value

    barrier = pltpu.get_barrier_semaphore()
    for devices in others:
        for device in devices:
            pl.semaphore_signal(barrier, inc=1, device_id=device, device_id_type=MESH)
    pl.semaphore_wait(barrier, sum(len(devices) for devices in others))

    offsets = [sum(halves[:p]) for p in range(count)]
    chunks = sum(halves) // CHUNK

    late = count - 1
    late_copies = []
    for j, peer in enumerate(peers):
        for c in range(late_pieces):
            rows = halves[late] // late_pieces
            late_copies.append(
                pltpu.make_async_remote_copy(
                    src_ref=full[late].at[pl.ds(peer * halves[late] + c * rows, rows)],
                    dst_ref=rc.at[j, pl.ds(offsets[late] + c * rows, rows)],
                    send_sem=late_send.at[j * late_pieces + c],
                    recv_sem=late_recv.at[j * late_pieces + c],
                    device_id=at(place, peer),
                    device_id_type=MESH,
                )
            )
    for copy in late_copies:
        copy.start()

    loads = []
    for p in range(count):
        one = [(full[p].at[pl.ds(side * halves[p], halves[p])], loc.at[pl.ds(offsets[p], halves[p])])]
        if p < early:
            for j in range(inner - 1):
                one.append((got[p].at[j], rc.at[j, pl.ds(offsets[p], halves[p])]))
        loads.append(
            [pltpu.make_async_copy(a, b, load.at[p * inner + i]) for i, (a, b) in enumerate(one)]
        )
    for one in loads:
        for copy in one:
            copy.start()
    small_round(0)

    def to_beside(src, dst, send, recv, t):
        rows = pl.ds(t * CHUNK, CHUNK)
        return pltpu.make_async_remote_copy(
            src_ref=src.at[rows], dst_ref=dst.at[rows], send_sem=send.at[t], recv_sem=recv.at[t],
            device_id=at(beside, side), device_id_type=MESH,
        )

    def to_across(t):
        rows = pl.ds(t * CHUNK, CHUNK)
        return pltpu.make_async_remote_copy(
            src_ref=loc.at[rows], dst_ref=rb2.at[rows], send_sem=s2.at[t], recv_sem=r2.at[t],
            device_id=at(across, side), device_id_type=MESH,
        )

    def to_peer(j, t):
        rows = pl.ds(t * CHUNK, CHUNK)
        return pltpu.make_async_remote_copy(
            src_ref=tot.at[rows], dst_ref=out.at[side, rows], send_sem=s4.at[j, t], recv_sem=r4.at[j, t],
            device_id=at(place, peers[j]), device_id_type=MESH,
        )

    def to_self(t):
        rows = pl.ds(t * CHUNK, CHUNK)
        return pltpu.make_async_copy(tot.at[rows], out.at[side, rows], keep.at[t])

    def hand_out(t):
        for j in range(inner - 1):
            to_peer(j, t).start()
        to_self(t).start()

    def step(t, carry):
        rows = pl.ds(pl.multiple_of(t * CHUNK, CHUNK), CHUNK)

        for i in range(1, len(rounds) + 1):

            @pl.when(t == 2 * i)
            def _(i=i):
                small_round(i)

        @pl.when(t < chunks)
        def _():
            for p in range(count):

                @pl.when(t == offsets[p] // CHUNK)
                def _(p=p):
                    for copy in loads[p]:
                        copy.wait()

            for c in range(late_pieces):

                @pl.when(t == (offsets[late] + c * (halves[late] // late_pieces)) // CHUNK)
                def _(c=c):
                    for j in range(inner - 1):
                        late_copies[j * late_pieces + c].wait_recv()

            total = loc[rows].astype(F32)
            for j in range(inner - 1):
                total += rc[j, rows].astype(F32)
            loc[rows] = total.astype(LOW)

            @pl.when(outside)
            def _():
                to_beside(loc, rb1, s1, r1, t).start()

            @pl.when(inside)
            def _():
                to_beside(loc, rb1, s1, r1, t).wait_recv()
                loc[rows] = (loc[rows].astype(F32) + rb1[rows].astype(F32)).astype(LOW)
                to_across(t).start()

        u = t - 1

        @pl.when(jnp.logical_and(inside, jnp.logical_and(u >= 0, u < chunks)))
        def _():
            ready = pl.ds(pl.multiple_of(u * CHUNK, CHUNK), CHUNK)
            to_across(u).wait_recv()
            tot[ready] = (loc[ready].astype(F32) + rb2[ready].astype(F32)).astype(LOW)
            to_beside(tot, tot, s3, r3, u).start()
            hand_out(u)

        w = t - LAG

        @pl.when(jnp.logical_and(outside, w >= 0))
        def _():
            to_beside(tot, tot, s3, r3, w).wait_recv()
            hand_out(w)

        return carry

    lax.fori_loop(0, chunks + LAG, step, 0)

    def finish(t, carry):
        @pl.when(outside)
        def _():
            to_beside(loc, rb1, s1, r1, t).wait_send()

        @pl.when(inside)
        def _():
            to_across(t).wait_send()
            to_beside(tot, tot, s3, r3, t).wait_send()

        for j in range(inner - 1):
            to_peer(j, t).wait()
        to_self(t).wait()
        return carry

    lax.fori_loop(0, chunks, finish, 0)
    for copy in late_copies:
        copy.wait_send()


LAG = 6


class Reducer:
    def __init__(self, mesh):
        self.inner = mesh.shape["dp"] // OUTER
        self.group = mesh.shape["mp"]

    def exchange(self, x):
        side = lax.rem(lax.axis_index("dp"), self.inner)
        rows = x.shape[0] // self.inner
        got = []
        for j in range(1, self.inner):
            pairs = []
            for o in range(OUTER):
                for i in range(self.inner):
                    pairs.append((o * self.inner + i, o * self.inner + (i + j) % self.inner))
            share = lax.dynamic_slice_in_dim(x, lax.rem(side + j, self.inner) * rows, rows)
            got.append(lax.ppermute(share, "dp", pairs))
        return jnp.stack(got)

    def reduce(self, pieces, got, small):
        inner = self.inner
        width = pieces[0].shape[1]
        halves = tuple(p.shape[0] // inner for p in pieces)
        share = sum(halves)
        chunks = share // CHUNK
        any_spec = pl.BlockSpec(memory_space=pl.ANY)
        late_pieces = halves[-1] // CHUNK // 2
        buffer = pltpu.VMEM((share, width), LOW)
        return pl.pallas_call(
            functools.partial(sum_kernel, inner, self.group, len(got), halves, late_pieces),
            out_shape=[
                jax.ShapeDtypeStruct((inner, share, width), LOW),
                jax.ShapeDtypeStruct(small.shape, F32),
            ],
            in_specs=[any_spec] * (len(pieces) + len(got)) + [pl.BlockSpec(memory_space=pltpu.VMEM)],
            out_specs=[any_spec, pl.BlockSpec(memory_space=pltpu.VMEM)],
            scratch_shapes=[
                buffer,
                pltpu.VMEM((inner - 1, share, width), LOW),
                buffer,
                buffer,
                buffer,
                sems(len(pieces) * inner),
                sems((inner - 1) * late_pieces),
                sems((inner - 1) * late_pieces),
                *[sems(chunks) for _ in range(6)],
                sems(inner - 1, chunks),
                sems(inner - 1, chunks),
                sems(chunks),
                pltpu.VMEM((self.group, *small.shape), F32),
                pltpu.VMEM((inner, *small.shape), F32),
                pltpu.VMEM((OUTER, *small.shape), F32),
                sems(self.group + inner + OUTER - 3),
                sems(self.group + inner + OUTER - 3),
            ],
            compiler_params=pltpu.CompilerParams(
                collective_id=0, has_side_effects=True, vmem_limit_bytes=VMEM_LIMIT
            ),
            cost_estimate=pl.CostEstimate(flops=0, bytes_accessed=600_000_000, transcendentals=0),
            name="sum_over_dp",
        )(*pieces, *got, small)


def body(
    mesh,
    rows,
    lengths,
    freq_class,
    freq_table,
    gain_attn,
    gain_mlp,
    w_qkv,
    w_out,
    w_gate_up,
    w_down,
    cotangent,
):
    reducer = Reducer(mesh)
    group_size = mesh.shape["mp"]
    chips = group_size // 2
    local_rows, d = rows.shape
    own_series = local_rows // SEQ
    mp_index = lax.axis_index("mp")
    heads_width = w_out.shape[0]
    head_count = heads_width // HS
    ff = w_down.shape[0]

    places = jnp.arange(group_size, dtype=jnp.int32)
    owners = ((mp_index // 2 + places // 2) % chips) * 2 + (mp_index % 2 + places) % 2
    starts = (SEQ - lengths.reshape(group_size, own_series))[owners]
    tables = slot_tables()
    slots = jnp.arange(SEQ, dtype=jnp.int32)
    mine_valid = (slots[None, :] >= starts[0][:, None]).astype(F32)
    starts = starts.reshape(-1)

    by_series = lambda v: v.reshape(own_series, SEQ, d)
    picked = freq_table[NFREQ - 1][None]
    for f in range(NFREQ - 1):
        picked = jnp.where((freq_class == f)[:, None], freq_table[f][None], picked)
    start_rows = (by_series(rows) + picked[:, None]).reshape(local_rows, d)
    inverse = lax.rsqrt(jnp.mean(start_rows * start_rows, -1, keepdims=True) + EPSILON)
    normed_mine = (start_rows * inverse * gain_attn).astype(LOW)
    grad_output = (by_series(cotangent) * mine_valid[:, :, None]).reshape(local_rows, d)

    selector = head_selector(head_count)
    qkv_low = jnp.einsum("cdf,fg->cdg", w_qkv.astype(LOW), selector, preferred_element_type=F32).astype(LOW)
    out_low = dot(selector, w_out.astype(LOW), 0, 0).astype(LOW)
    gate_low = w_gate_up[0].astype(LOW)
    up_low = w_gate_up[1].astype(LOW)
    down_low = w_down.astype(LOW)

    qkv, mixed, normed, after_attn, normed_mlp_mine = attn_forward(
        chips, normed_mine, start_rows, gain_mlp[None], qkv_low, out_low, starts, tables
    )
    hidden, grad_pre, normed_mlp, grad_down_in, down_own, down_far, grad_after, grad_after_low, gains_mlp = mlp_both(
        chips, normed_mlp_mine, grad_output.astype(LOW), after_attn, grad_output, gain_mlp[None],
        gate_low, up_low, down_low,
    )
    flat = lambda v: v.reshape(-1, d)
    grad_down = weight_grad([hidden], [flat(grad_down_in)])
    ups = [weight_grad([flat(normed_mlp)], [grad_pre], c) for c in range(2)]
    pieces = [grad_down] + (ups if ff >= d else [jnp.concatenate(ups, 1)])
    got = [reducer.exchange(p) for p in pieces]
    output = after_attn + down_own.astype(F32)
    for k in range(1, chips):
        far = lax.ppermute(down_far[k - 1], "mp", [(i, (i + 2 * k) % group_size) for i in range(group_size)])
        output += far.astype(F32)

    grad_proj, grad_attn_in, grad_rows, gains_attn = attn_backward(
        chips, grad_after_low, start_rows, grad_after, gain_attn[None], qkv, qkv_low, out_low, starts, tables
    )
    pieces.append(
        attn_weight_grad([grad_proj], [mixed], [flat(normed)], [flat(grad_attn_in)], selector)
    )
    series_sums = jnp.sum(by_series(grad_rows), 1)
    grad_table = [jnp.sum(jnp.where((freq_class == f)[:, None], series_sums, 0.0), 0) for f in range(NFREQ)]

    tokens = jnp.full((d,), jnp.sum(mine_valid))
    zero = jnp.zeros((d,), F32)
    small = jnp.stack([gains_attn[0], gains_mlp[0], *grad_table, tokens, zero, zero])
    sums, small = reducer.reduce(pieces, got, small)
    root_scale = lax.rsqrt(small[2 + NFREQ, 0])
    small = small * root_scale
    finals, offset = [], 0
    for piece in pieces:
        share = piece.shape[0] // reducer.inner
        finals.append(sums[:, offset : offset + share].reshape(piece.shape))
        offset += share
    down_out = finals[0].astype(F32) * root_scale
    if len(finals) == 3:
        gate_up_out = jnp.stack([finals[1][:, :ff], finals[1][:, ff:]]).astype(F32) * root_scale
    else:
        gate_up_out = jnp.stack(finals[1:3]).astype(F32) * root_scale
    identity = jnp.eye(heads_width, dtype=LOW)
    last = finals[-1]
    qkv_out = jnp.stack(
        [dot(last[c * heads_width : (c + 1) * heads_width], identity, 0, 0) * root_scale for c in range(3)]
    )
    out_out = last[3 * heads_width :].astype(F32) * root_scale
    return (
        output,
        grad_rows,
        qkv_out,
        out_out,
        gate_up_out,
        down_out,
        small[0],
        small[1],
        small[2 : 2 + NFREQ],
    )


def solution(mesh):
    return jax.shard_map(
        functools.partial(body, mesh),
        mesh=mesh,
        in_specs=(
            P(("dp", "mp"), None),
            P("dp"),
            P(("dp", "mp")),
            P(),
            P(),
            P(),
            P(None, None, "mp"),
            P("mp", None),
            P(None, None, "mp"),
            P("mp", None),
            P(("dp", "mp"), None),
        ),
        out_specs=(
            P(("dp", "mp"), None),
            P(("dp", "mp"), None),
            P(None, None, "mp"),
            P("mp", None),
            P(None, None, "mp"),
            P("mp", None),
            P(),
            P(),
            P(),
        ),
        check_vma=False,
    )
```

```python
import functools

import jax
import jax.numpy as jnp
import numpy as np
from jax import lax
from jax.experimental import pallas as pl
from jax.experimental.pallas import tpu as pltpu
from jax.sharding import PartitionSpec as P

HS = 80
HALF = HS // 2
LANES = 128
NFREQ = 3
SEQ = 64
BLOCK = 256
PAIR = 128

EPSILON = 1e-06
NEGATIVE = -1e30
HIGHEST = lax.Precision.HIGHEST
LOW = jnp.bfloat16
F32 = jnp.float32
VMEM_LIMIT = 62 * 1024 * 1024 + 512 * 1024
MESH = pl.DeviceIdType.MESH
LN2 = float(np.log(2.0))
QSCALE = float(HS**-0.5 / np.log(2.0))


def dot(a, b, ca=1, cb=0):
    return lax.dot_general(a, b, (((ca,), (cb,)), ((), ())), preferred_element_type=F32)


def head_selector(head_count):
    sel = np.zeros((head_count * HS, head_count * LANES), np.float32)
    for h in range(head_count):
        for half in range(2):
            for i in range(HALF):
                sel[h * HS + half * HALF + i, h * LANES + half * (LANES // 2) + i] = 1.0
    return jnp.asarray(sel, LOW)


def slot_tables():
    frequency = 10000.0 ** (-2.0 * np.arange(HALF) / HS)
    angles = np.arange(SEQ)[:, None] * frequency[None, :]
    pad = ((0, 0), (0, LANES // 2 - HALF))
    cosines = np.pad(np.cos(angles), pad)
    sines = np.pad(np.sin(angles), pad)
    return (
        jnp.asarray(np.concatenate([cosines, cosines], 1), F32),
        jnp.asarray(np.concatenate([-sines, sines], 1), F32),
    )


def row_angles(cp, sp, starts, first, count):
    cosines, sines = [], []
    c, s = cp[...], sp[...]
    for i in range(count):
        start = pl.ds(starts[first + i], 1)
        c0, s0 = cp[start, :], sp[start, :]
        cosines.append(c * c0 + s * s0)
        sines.append(s * c0 - c * s0)
    return jnp.concatenate(cosines, 0), jnp.concatenate(sines, 0)


def pair_mask(starts, first):
    j = lax.broadcasted_iota(jnp.int32, (PAIR, PAIR), 0)
    i = lax.broadcasted_iota(jnp.int32, (PAIR, PAIR), 1)
    begin = jnp.where(j < SEQ, starts[first], SEQ + starts[first + 1])
    same = (j < SEQ) == (i < SEQ)
    allowed = (same & (j <= i) & (j >= begin)) | (j == i)
    return jnp.where(allowed, 0.0, NEGATIVE)


def softmax_down(scores):
    exponent = jnp.exp2(scores - jnp.max(scores, 0, keepdims=True))
    return exponent * (1.0 / jnp.sum(exponent, 0, keepdims=True))


class Links:
    def __init__(self, chips, blocks, rb):
        self.chips, self.blocks, self.rb = chips, blocks, rb
        self.n = 2 * chips
        self.dp, self.mp = lax.axis_index("dp"), lax.axis_index("mp")
        self.core = (self.dp, self.mp + 1 - 2 * lax.rem(self.mp, 2))

    def further(self, k):
        return (self.dp, lax.rem(self.mp + 2 * k, self.n))

    def nearer(self, k):
        return (self.dp, lax.rem(self.mp + 2 * (self.chips - k), self.n))

    def greet(self):
        barrier = pltpu.get_barrier_semaphore()
        for j in range(1, self.n):
            other = (self.dp, lax.rem(self.mp + j, self.n))
            pl.semaphore_signal(barrier, inc=1, device_id=other, device_id_type=MESH)
        pl.semaphore_wait(barrier, self.n - 1)

    def rows(self, b):
        return pl.ds(b * self.rb, self.rb)

    def block(self, k, s, b):
        at = (2 * k + s) * (self.blocks * self.rb) + b * self.rb
        return pl.ds(at if isinstance(at, int) else pl.multiple_of(at, self.rb), self.rb)

    def each(self, body):
        def one(q, carry):
            body(q // self.blocks, lax.rem(q, self.blocks))
            return carry

        lax.fori_loop(0, self.chips * self.blocks, one, 0)


def remote(src, dst, send, recv, device):
    return pltpu.make_async_remote_copy(
        src_ref=src, dst_ref=dst, send_sem=send, recv_sem=recv, device_id=device, device_id_type=MESH
    )


class Gather:
    def __init__(self, links, x, buf, local, core_send, core_recv, chip_send, chip_recv):
        self.links, self.x, self.buf, self.local = links, x, buf, local
        self.core_send, self.core_recv = core_send, core_recv
        self.chip_send, self.chip_recv = chip_send, chip_recv

    def place(self, k, s, b):
        return self.buf.at[self.links.block(k, s, b)]

    def own(self, b):
        return pltpu.make_async_copy(self.x.at[self.links.rows(b)], self.place(0, 0, b), self.local.at[b])

    def to_chip(self, k, b):
        rows = self.links.rows(b)
        return remote(
            self.x.at[rows], self.place(k, 0, b), self.chip_send.at[k, b], self.chip_recv.at[k, b],
            self.links.nearer(k),
        )

    def to_core(self, k, b):
        return remote(
            self.place(k, 0, b), self.place(k, 1, b), self.core_send.at[k, b], self.core_recv.at[k, b],
            self.links.core,
        )

    def own_to_core(self, b):
        rows = self.links.rows(b)
        return remote(
            self.x.at[rows], self.place(0, 1, b), self.core_send.at[0, b], self.core_recv.at[0, b],
            self.links.core,
        )

    def start_near(self):
        for b in range(self.links.blocks):
            self.own(b).start()
            self.own_to_core(b).start()

    def start_far(self, b):
        for k in range(1, self.links.chips):
            self.to_chip(k, b).start()

    def arrive(self, k, b, second):
        @pl.when(jnp.logical_and(jnp.logical_not(second), k == 0))
        def _():
            self.own(b).wait()

        @pl.when(jnp.logical_and(jnp.logical_not(second), k > 0))
        def _():
            self.to_chip(k, b).wait_recv()
            self.to_core(k, b).start()

        @pl.when(second)
        def _():
            self.to_core(k, b).wait_recv()

    def finish(self):
        def sent(k, b):
            self.to_core(k, b).wait_send()

            @pl.when(k > 0)
            def _():
                self.to_chip(k, b).wait_send()

        self.links.each(sent)

    @staticmethod
    def scratch(chips, blocks):
        return [pltpu.SemaphoreType.DMA((blocks,))] + [pltpu.SemaphoreType.DMA((chips, blocks))] * 4


class Scatter:
    def __init__(self, links, give, keep, got, far, core_send, core_recv, chip_send, chip_recv):
        self.links, self.give, self.keep, self.got, self.far = links, give, keep, got, far
        self.core_send, self.core_recv = core_send, core_recv
        self.chip_send, self.chip_recv = chip_send, chip_recv

    def to_core(self, k, b):
        rows = self.links.rows(b)
        return remote(
            self.give.at[k, rows], self.got.at[k, rows], self.core_send.at[k, b], self.core_recv.at[k, b],
            self.links.core,
        )

    def to_chip(self, k, b):
        rows = self.links.rows(b)
        return remote(
            self.keep.at[k, rows], self.far.at[k - 1, rows], self.chip_send.at[k, b], self.chip_recv.at[k, b],
            self.links.further(k),
        )

    def put(self, k, b, second, value):
        rows = self.links.rows(b)

        @pl.when(jnp.logical_not(second))
        def _():
            self.keep[k, rows] = value.astype(LOW)

        @pl.when(second)
        def _():
            self.give[k, rows] = value.astype(LOW)
            self.to_core(k, b).start()

    def pair_done(self, k, b):
        rows = self.links.rows(b)
        self.to_core(k, b).wait_recv()

        @pl.when(k > 0)
        def _():
            self.keep[k, rows] = (self.keep[k, rows].astype(F32) + self.got[k, rows].astype(F32)).astype(LOW)
            self.to_chip(k, b).start()

    def total(self, b):
        rows = self.links.rows(b)
        value = self.keep[0, rows].astype(F32) + self.got[0, rows].astype(F32)
        for k in range(1, self.links.chips):
            self.to_chip(k, b).wait_recv()
            value += self.far[k - 1, rows].astype(F32)
        return value

    def finish(self):
        def sent(k, b):
            self.to_core(k, b).wait_send()

            @pl.when(k > 0)
            def _():
                self.to_chip(k, b).wait_send()

        self.links.each(sent)

    @staticmethod
    def scratch(chips, blocks, rows, width):
        buffers = [pltpu.VMEM((n, rows, width), LOW) for n in (chips, chips, chips, chips - 1)]
        return buffers + [pltpu.SemaphoreType.DMA((chips, blocks))] * 4


def run_blocks(links, arrive, compute, scatters):
    def step(i, carry):
        q, second = i // 2, lax.rem(i, 2) == 1
        k, b = q // links.blocks, lax.rem(q, links.blocks)
        arrive(i, k, b, second)
        for scatter, value in zip(scatters, compute(i, k, b, second)):
            scatter.put(k, b, second, value)

        @pl.when(jnp.logical_and(jnp.logical_not(second), q > 0))
        def _():
            for scatter in scatters:
                scatter.pair_done((q - 1) // links.blocks, lax.rem(q - 1, links.blocks))

        return carry

    pairs = links.chips * links.blocks
    lax.fori_loop(0, 2 * pairs, step, 0)
    for scatter in scatters:
        scatter.pair_done(links.chips - 1, links.blocks - 1)


class Store:
    def __init__(self, sems, pairs):
        self.sems, self.pairs = sems, pairs

    def copies(self, i):
        return [pltpu.make_async_copy(a, b, self.sems.at[i, j]) for j, (a, b) in enumerate(self.pairs(i))]

    def start(self, i):
        for copy in self.copies(i):
            copy.start()

    def wait(self, i):
        for copy in self.copies(i):
            copy.wait()


def loader(sems, pairs):
    copies = [pltpu.make_async_copy(a, b, sems.at[i]) for i, (a, b) in enumerate(pairs)]
    for copy in copies:
        copy.start()
    return copies


def step_place(links, i):
    q, s = i // 2, lax.rem(i, 2)
    return q // links.blocks, s, lax.rem(q, links.blocks)


def valid_rows(starts, first, rows):
    slot = lax.broadcasted_iota(jnp.int32, (SEQ, 1), 0)
    return jnp.concatenate(
        [(slot >= starts[first + i]).astype(F32) for i in range(rows // SEQ)], 0
    )


def with_class_rows(begin, picked):
    for i in range(begin.shape[0] // SEQ):
        begin[i * SEQ : (i + 1) * SEQ] += picked[i : i + 1]


def norm_low(value, gain):
    inverse = lax.rsqrt(jnp.mean(value * value, -1, keepdims=True) + EPSILON)
    return (value * inverse * gain).astype(LOW)


def cast_rows(src, dst, wide, low, load, store):
    tile = wide.shape[1]
    count = src.shape[0] // tile

    def get(t):
        return pltpu.make_async_copy(src.at[pl.ds(t * tile, tile)], wide.at[lax.rem(t, 2)], load.at[lax.rem(t, 2)])

    def give(t):
        return pltpu.make_async_copy(low.at[lax.rem(t, 2)], dst.at[pl.ds(t * tile, tile)], store.at[lax.rem(t, 2)])

    get(0).start()

    def one(t, carry):
        @pl.when(t + 1 < count)
        def _():
            get(t + 1).start()

        get(t).wait()

        @pl.when(t >= 2)
        def _():
            give(t - 2).wait()

        low[lax.rem(t, 2)] = wide[lax.rem(t, 2)].astype(LOW)
        give(t).start()
        return carry

    lax.fori_loop(0, count, one, 0)
    for t in range(max(count - 2, 0), count):
        give(t).wait()


def attn_fwd_kernel(
    nh, chips, blocks, rb, rows_any, cot_any, picked, gain_attn, gain_mlp, wqkv_any, wout_any, gate_any, down_any,
    selector, starts, cp, sp, *refs
):
    qkv_out, mixed_out, xg_out, wqkv_out, wout_out, gate_out, down_out, after, normed, gy, refs = *refs[:10], refs[10:]
    x, xg, wqkv, wout, wqkv_wide, wout_wide, qkv, mixed, begin, cot, load, store_sems, refs = *refs[:12], refs[12:]
    gate_wide, gate_low, down_wide, down_low, cast_sems, weight_sems, refs = *refs[:6], refs[6:]
    gather_refs, scatter_refs = refs[:5], refs[5:]
    links = Links(chips, blocks, rb)
    loads = loader(
        load, [(rows_any, begin), (wqkv_any, wqkv_wide), (wout_any, wout_wide), (cot_any, cot)]
    )
    loads[0].wait()
    with_class_rows(begin, picked)
    for b in range(blocks):
        x[b * rb : (b + 1) * rb] = norm_low(begin[b * rb : (b + 1) * rb], gain_attn[...])
    links.greet()
    gather = Gather(links, x, xg, *gather_refs)
    scatter = Scatter(links, *scatter_refs)
    for b in range(blocks):
        gather.start_far(b)
    gather.start_near()
    width = nh * LANES
    series = rb // SEQ
    loads[1].wait()
    for c in range(3):
        wqkv[c] = dot(wqkv_wide[c].astype(LOW), selector[...]).astype(LOW)
    loads[2].wait()
    wout[...] = dot(selector[...], wout_wide[...].astype(LOW), 0, 0).astype(LOW)
    weights = loader(weight_sems, [(wqkv, wqkv_out), (wout, wout_out)])

    def pairs(i):
        rows = links.block(*step_place(links, i))
        return [
            (qkv.at[rows], qkv_out.at[rows]),
            (mixed.at[rows], mixed_out.at[rows]),
            (xg.at[rows], xg_out.at[rows]),
        ]

    store = Store(store_sems, pairs)

    def compute(i, k, b, second):
        rows = links.block(*step_place(links, i))
        at = rows.start
        first = at // SEQ
        xs = xg[rows]
        c, sn = row_angles(cp, sp, starts, first, series)
        for part in range(3):
            proj = dot(xs, wqkv[part])
            if part == 2:
                qkv[rows, 2 * width :] = proj.astype(LOW)
                continue
            scale = QSCALE if part == 0 else 1.0
            cc, ss = c * scale, sn * scale
            for h in range(nh):
                p = proj[:, h * LANES : (h + 1) * LANES]
                cols = slice(part * width + h * LANES, part * width + (h + 1) * LANES)
                qkv[rows, cols] = (p * cc + pltpu.roll(p, LANES // 2, 1) * ss).astype(LOW)
        for p in range(rb // PAIR):
            sub = pl.ds(pl.multiple_of(at + p * PAIR, PAIR), PAIR)
            mask = pair_mask(starts, first + 2 * p)
            get = lambda part, h: qkv[sub, part * width + h * LANES : part * width + (h + 1) * LANES]
            scores = [dot(get(1, h), get(0, h), 1, 1) + mask for h in range(nh)]
            attention = [softmax_down(v).astype(LOW) for v in scores]
            for h in range(nh):
                mixed[sub, h * LANES : (h + 1) * LANES] = dot(attention[h], get(2, h), 0, 0).astype(LOW)
        part = dot(mixed[rows], wout[...])
        store.start(i)
        return [part]

    run_blocks(links, lambda i, k, b, second: gather.arrive(k, b, second), compute, [scatter])

    loads[3].wait()
    for b in range(blocks):
        rows = slice(b * rb, (b + 1) * rb)
        gy[rows] = (cot[rows] * valid_rows(starts, b * series, rb)).astype(LOW)
    cast_rows(gate_any, gate_out, gate_wide, gate_low, cast_sems.at[0], cast_sems.at[1])
    cast_rows(down_any, down_out, down_wide, down_low, cast_sems.at[2], cast_sems.at[3])
    for b in range(blocks):
        rows = slice(b * rb, (b + 1) * rb)
        value = begin[rows] + scatter.total(b)
        after[rows] = value
        normed[rows] = norm_low(value, gain_mlp[...])
    gather.finish()
    scatter.finish()
    for copy in weights:
        copy.wait()

    def stored(i, carry):
        store.wait(i)
        return carry

    lax.fori_loop(0, 2 * chips * blocks, stored, 0)


def norm_backward_block(value, gain, grad_normed, before):
    inverse = lax.rsqrt(jnp.mean(value * value, -1, keepdims=True) + EPSILON)
    normal = value * inverse
    scaled = grad_normed * gain
    grad = before + inverse * (scaled - normal * jnp.mean(scaled * normal, -1, keepdims=True))
    return grad, jnp.sum(grad_normed * normal, 0, keepdims=True)


def column_tiles(body, width, tile, stage, sems, copies):
    def start_all(t, wait):
        cols = pl.ds(pl.multiple_of(t * tile, tile), tile)
        slot = lax.rem(t, 2)
        for j, (a, b) in enumerate(copies(slot, cols)):
            copy = pltpu.make_async_copy(a, b, sems.at[slot, j])
            if wait:
                copy.wait()
            else:
                copy.start()

    count = width // tile

    def one(t, carry):
        @pl.when(t >= 2)
        def _():
            start_all(t - 2, True)

        body(lax.rem(t, 2), pl.ds(pl.multiple_of(t * tile, tile), tile))
        start_all(t, False)
        return carry

    lax.fori_loop(0, count, one, 0)
    for t in range(max(count - 2, 0), count):
        start_all(t, True)


def mlp_kernel(chips, inner, blocks, rb, x, gy, after, cot, gain, gate_any, down_any, starts, *refs):
    gpre_out, xg_out, own_out, far_out, refs = *refs[:4], refs[4:]
    grad_down, refs = refs[:inner], refs[inner:]
    grad_after, low_after, gain_grad, refs = *refs[:3], refs[3:]
    xg, yg, wgate, wup, wdown, hidden, gpre, begin, before, stage, load, store_sems, refs = *refs[:12], refs[12:]
    down_sems, stage_sems, refs = *refs[:2], refs[2:]
    xg_refs, yg_refs, back_refs = refs[:5], refs[5:10], refs[10:18]
    give, keep, got, down_send, down_recv = refs[18:]
    d, ff = wgate.shape
    links = Links(chips, blocks, rb)
    loads = loader(
        load,
        [
            (gate_any.at[pl.ds(0, d)], wgate),
            (gate_any.at[pl.ds(d, d)], wup),
            (down_any, wdown),
            (after, begin),
            (cot, before),
        ],
    )
    links.greet()
    gather = Gather(links, x, xg, *xg_refs)
    second_gather = Gather(links, gy, yg, *yg_refs)
    back = Scatter(links, *back_refs)
    for b in range(blocks):
        gather.start_far(b)
    gather.start_near()
    second_gather.start_near()

    def down_to_core(k, b):
        rows = links.rows(b)
        return remote(
            give.at[k, rows], got.at[k, rows], down_send.at[k, b], down_recv.at[k, b], links.core
        )

    def pairs(i):
        rows = links.block(*step_place(links, i))
        slot = lax.rem(i, 2)
        return [
            (gpre.at[slot, 0], gpre_out.at[0, rows]),
            (gpre.at[slot, 1], gpre_out.at[1, rows]),
            (xg.at[rows], xg_out.at[rows]),
        ]

    store = Store(store_sems, pairs)
    steps = 2 * chips * blocks

    def arrive(i, k, b, second):
        for j in range(blocks):

            @pl.when(i == min(blocks + j, 2 * blocks - 1))
            def _(j=j):
                second_gather.start_far(j)

        gather.arrive(k, b, second)

        @pl.when(i == 0)
        def _():
            loads[0].wait()
            loads[1].wait()
            loads[2].wait()

    def compute(i, k, b, second):
        block = links.block(*step_place(links, i))
        slot = lax.rem(i, 2)

        @pl.when(i >= 2)
        def _():
            store.wait(i - 2)

        xs = xg[block]
        gate = dot(xs, wgate[...])
        sig = jax.nn.sigmoid(gate)
        act = gate * sig
        slope = sig * (1.0 + gate * (1.0 - sig))
        up = dot(xs, wup[...])
        hidden[block] = (act * up).astype(LOW)
        second_gather.arrive(k, b, second)
        gh = dot(yg[block], wdown[...], 1, 1)
        gpre[slot, 0] = (gh * up * slope).astype(LOW)
        gpre[slot, 1] = (gh * act).astype(LOW)
        grad = dot(gpre[slot, 0], wgate[...], 1, 1) + dot(gpre[slot, 1], wup[...], 1, 1)
        down = dot(hidden[block], wdown[...]).astype(LOW)
        rows = links.rows(b)

        @pl.when(jnp.logical_not(second))
        def _():
            keep[k, rows] = down

        @pl.when(second)
        def _():
            give[k, rows] = down
            down_to_core(k, b).start()

        store.start(i)
        return [grad]

    run_blocks(links, arrive, compute, [back])

    def down_sum(k, b):
        rows = links.rows(b)
        down_to_core(k, b).wait_recv()
        keep[k, rows] = (keep[k, rows].astype(F32) + got[k, rows].astype(F32)).astype(LOW)

    links.each(down_sum)
    outs = [pltpu.make_async_copy(keep.at[0], own_out, down_sems.at[0])]
    for k in range(1, chips):
        outs.append(pltpu.make_async_copy(keep.at[k], far_out.at[k - 1], down_sems.at[k]))
    for copy in outs:
        copy.start()

    side = lax.rem(lax.axis_index("dp"), inner)
    share = ff // inner

    def down_grad(slot, cols):
        stage[slot] = dot(hidden[...], yg[:, cols], 0, 0).astype(LOW)

    def shares(slot, cols):
        return [
            (stage.at[slot, pl.ds(lax.rem(side + j, inner) * share, share)], grad_down[j].at[:, cols])
            for j in range(inner)
        ]

    column_tiles(down_grad, d, stage.shape[2], stage, stage_sems, shares)
    loads[3].wait()
    loads[4].wait()
    gain_grad[...] = jnp.zeros_like(gain_grad)
    for b in range(blocks):
        rows = slice(b * rb, (b + 1) * rb)
        grad_out = before[rows] * valid_rows(starts, b * (rb // SEQ), rb)
        grad, gains = norm_backward_block(begin[rows], gain[...], back.total(b), grad_out)
        begin[rows] = grad
        yg[rows] = grad.astype(LOW)
        for j, (a, to) in enumerate([(begin, grad_after), (yg, low_after)]):
            at = pl.ds(b * rb, rb)
            outs.append(pltpu.make_async_copy(a.at[at], to.at[at], down_sems.at[chips + 2 * b + j]))
            outs[-1].start()
        gain_grad[0:1] += gains
    gather.finish()
    second_gather.finish()
    back.finish()
    links.each(lambda k, b: down_to_core(k, b).wait_send())
    for copy in outs:
        copy.wait()
    store.wait(steps - 2)
    store.wait(steps - 1)


def attn_bwd_kernel(
    nh, chips, blocks, rb, x, rows_any, before_any, picked, gain, qkv_any, mixed_any, normed_any, wqkv_any, wout_any,
    selector, starts, cp, sp, *refs
):
    late_out, grad_rows, gain_grad, series_grad, refs = *refs[:4], refs[4:]
    xg, wqkv, wout, qkv, mixed, normed, gproj, gmix, begin, before, stage, load, stage_sems, refs = *refs[:13], refs[13:]
    gather_refs, scatter_refs = refs[:5], refs[5:]
    links = Links(chips, blocks, rb)
    loads = loader(
        load,
        [
            (wout_any, wout),
            (qkv_any, qkv),
            (wqkv_any, wqkv),
            (rows_any, begin),
            (before_any, before),
            (mixed_any, mixed),
            (normed_any, normed),
        ],
    )
    links.greet()
    gather = Gather(links, x, xg, *gather_refs)
    scatter = Scatter(links, *scatter_refs)
    for b in range(blocks):
        gather.start_far(b)
    gather.start_near()
    for copy in loads[:3]:
        copy.wait()
    width = nh * LANES
    series = rb // SEQ
    real, d = selector.shape[0], xg.shape[1]

    def compute(i, k, b, second):
        rows = links.block(*step_place(links, i))
        at = rows.start
        first = at // SEQ
        gmix[...] = dot(xg[rows], wout[...], 1, 1).astype(LOW)
        c, sn = row_angles(cp, sp, starts, first, series)
        qc, qs = c * HS ** (-0.5), sn * HS ** (-0.5)
        kc, ks = c * LN2, sn * LN2
        for p in range(rb // PAIR):
            part = slice(p * PAIR, (p + 1) * PAIR)
            sub = pl.ds(pl.multiple_of(at + p * PAIR, PAIR), PAIR)
            mask = pair_mask(starts, first + 2 * p)
            col = lambda part, h: slice(part * width + h * LANES, part * width + (h + 1) * LANES)
            heads = range(nh)
            gm = [gmix[part, col(0, h)] for h in heads]
            scores = [dot(qkv[sub, col(1, h)], qkv[sub, col(0, h)], 1, 1) + mask for h in heads]
            grads = [dot(qkv[sub, col(2, h)], gm[h], 1, 1) for h in heads]
            attention = [softmax_down(v) for v in scores]
            for h in heads:
                gproj[sub, col(2, h)] = dot(attention[h].astype(LOW), gm[h]).astype(LOW)
            low = []
            for h in heads:
                both = attention[h] * grads[h]
                low.append((both - attention[h] * jnp.sum(both, 0, keepdims=True)).astype(LOW))
            for h in heads:
                g = dot(low[h], qkv[sub, col(0, h)])
                gproj[sub, col(1, h)] = (g * kc[part] - pltpu.roll(g, LANES // 2, 1) * ks[part]).astype(LOW)
            for h in heads:
                g = dot(low[h], qkv[sub, col(1, h)], 0, 0)
                gproj[sub, col(0, h)] = (g * qc[part] - pltpu.roll(g, LANES // 2, 1) * qs[part]).astype(LOW)
        value = dot(gproj[rows, :width], wqkv[0], 1, 1)
        value += dot(gproj[rows, width : 2 * width], wqkv[1], 1, 1)
        value += dot(gproj[rows, 2 * width :], wqkv[2], 1, 1)
        return [value]

    run_blocks(links, lambda i, k, b, second: gather.arrive(k, b, second), compute, [scatter])
    for copy in loads[3:]:
        copy.wait()

    def projections(slot, cols):
        for c in range(4):
            if c < 3:
                grad = dot(gproj[:, c * width : (c + 1) * width], normed[:, cols], 0, 0)
            else:
                grad = dot(mixed[...], xg[:, cols], 0, 0)
            stage[slot, c * real : (c + 1) * real] = dot(selector[...], grad.astype(LOW)).astype(LOW)

    column_tiles(
        projections, d, stage.shape[2], stage, stage_sems,
        lambda slot, cols: [(stage.at[slot], late_out.at[:, cols])],
    )
    with_class_rows(begin, picked)
    gain_grad[...] = jnp.zeros_like(gain_grad)
    for b in range(blocks):
        rows = slice(b * rb, (b + 1) * rb)
        grad, gains = norm_backward_block(begin[rows], gain[...], scatter.total(b), before[rows])
        grad_rows[rows] = grad
        gain_grad[0:1] += gains
        for i in range(series):
            series_grad[b * series + i : b * series + i + 1] = jnp.sum(
                grad[i * SEQ : (i + 1) * SEQ], 0, keepdims=True
            )
    gather.finish()
    scatter.finish()


def resident(shape):
    return pl.BlockSpec(shape, lambda i, *_: (0,) * len(shape), pipeline_mode=pl.Buffered(1))


def params(collective_id=None):
    return pltpu.CompilerParams(
        vmem_limit_bytes=VMEM_LIMIT, collective_id=collective_id, has_side_effects=collective_id is not None
    )


ANY = pl.BlockSpec(memory_space=pl.ANY)
WHOLE = pl.BlockSpec(memory_space=pltpu.VMEM)
SCALARS = pl.BlockSpec(memory_space=pltpu.SMEM)


def sems(*shape):
    return pltpu.SemaphoreType.DMA(shape)


def attn_forward(chips, rows, cot, picked, gain_attn, gain_mlp, w_qkv, w_out, w_gate_up, w_down, selector, starts, tables):
    r, d = rows.shape
    m = 2 * chips * r
    real, width = selector.shape
    ff = w_down.shape[0]
    nh = width // LANES
    rb = min(BLOCK, r)
    blocks = r // rb
    steps = 2 * chips * blocks
    tile = 128
    return pl.pallas_call(
        functools.partial(attn_fwd_kernel, nh, chips, blocks, rb),
        out_shape=[
            jax.ShapeDtypeStruct((m, 3 * width), LOW),
            jax.ShapeDtypeStruct((m, width), LOW),
            jax.ShapeDtypeStruct((m, d), LOW),
            jax.ShapeDtypeStruct((3, d, width), LOW),
            jax.ShapeDtypeStruct((width, d), LOW),
            jax.ShapeDtypeStruct((2 * d, ff), LOW),
            jax.ShapeDtypeStruct((ff, d), LOW),
            jax.ShapeDtypeStruct((r, d), F32),
            jax.ShapeDtypeStruct((r, d), LOW),
            jax.ShapeDtypeStruct((r, d), LOW),
        ],
        in_specs=[ANY, ANY, WHOLE, WHOLE, WHOLE, ANY, ANY, ANY, ANY, WHOLE, SCALARS, WHOLE, WHOLE],
        out_specs=[ANY] * 7 + [WHOLE] * 3,
        scratch_shapes=[
            pltpu.VMEM((r, d), LOW),
            pltpu.VMEM((m, d), LOW),
            pltpu.VMEM((3, d, width), LOW),
            pltpu.VMEM((width, d), LOW),
            pltpu.VMEM((3, d, real), F32),
            pltpu.VMEM((real, d), F32),
            pltpu.VMEM((m, 3 * width), LOW),
            pltpu.VMEM((m, width), LOW),
            pltpu.VMEM((r, d), F32),
            pltpu.VMEM((r, d), F32),
            sems(4),
            sems(steps, 3),
            pltpu.VMEM((2, tile, ff), F32),
            pltpu.VMEM((2, tile, ff), LOW),
            pltpu.VMEM((2, tile, d), F32),
            pltpu.VMEM((2, tile, d), LOW),
            sems(4, 2),
            sems(2),
            *Gather.scratch(chips, blocks),
            *Scatter.scratch(chips, blocks, r, d),
        ],
        compiler_params=params(1),
        name="attn_fwd",
    )(
        rows, cot, picked, gain_attn, gain_mlp, w_qkv, w_out, w_gate_up.reshape(2 * d, ff), w_down, selector,
        starts, *tables,
    )


def mlp_both(chips, inner, x, gy, after, cot, gain, gate_low, down_low, starts):
    r, d = x.shape
    m = 2 * chips * r
    ff = down_low.shape[0]
    rb = min(BLOCK, r)
    blocks = r // rb
    steps = 2 * chips * blocks
    tile = 256
    return pl.pallas_call(
        functools.partial(mlp_kernel, chips, inner, blocks, rb),
        out_shape=[
            jax.ShapeDtypeStruct((2, m, ff), LOW),
            jax.ShapeDtypeStruct((m, d), LOW),
            jax.ShapeDtypeStruct((r, d), LOW),
            jax.ShapeDtypeStruct((chips - 1, r, d), LOW),
            *[jax.ShapeDtypeStruct((ff // inner, d), LOW)] * inner,
            jax.ShapeDtypeStruct((r, d), F32),
            jax.ShapeDtypeStruct((r, d), LOW),
            jax.ShapeDtypeStruct((8, d), F32),
        ],
        in_specs=[ANY, ANY, ANY, ANY, WHOLE, ANY, ANY, SCALARS],
        out_specs=[ANY] * (6 + inner) + [WHOLE],
        scratch_shapes=[
            pltpu.VMEM((m, d), LOW),
            pltpu.VMEM((m, d), LOW),
            pltpu.VMEM((d, ff), LOW),
            pltpu.VMEM((d, ff), LOW),
            pltpu.VMEM((ff, d), LOW),
            pltpu.VMEM((m, ff), LOW),
            pltpu.VMEM((2, 2, rb, ff), LOW),
            pltpu.VMEM((r, d), F32),
            pltpu.VMEM((r, d), F32),
            pltpu.VMEM((2, ff, tile), LOW),
            sems(5),
            sems(steps, 3),
            sems(chips + 2 * blocks),
            sems(2, inner),
            *Gather.scratch(chips, blocks),
            *Gather.scratch(chips, blocks),
            *Scatter.scratch(chips, blocks, r, d),
            *[pltpu.VMEM((chips, r, d), LOW)] * 3,
            sems(chips, blocks),
            sems(chips, blocks),
        ],
        compiler_params=params(2),
        name="mlp_both",
    )(x, gy, after, cot, gain, gate_low, down_low, starts)


def attn_backward(
    chips, x, rows, before, picked, gain, qkv, mixed, normed, wqkv, wout, selector, starts, tables
):
    r, d = x.shape
    m = 2 * chips * r
    real, width = selector.shape
    nh = width // LANES
    rb = min(BLOCK, r)
    blocks = r // rb
    tile = 256
    return pl.pallas_call(
        functools.partial(attn_bwd_kernel, nh, chips, blocks, rb),
        out_shape=[
            jax.ShapeDtypeStruct((4 * real, d), LOW),
            jax.ShapeDtypeStruct((r, d), F32),
            jax.ShapeDtypeStruct((8, d), F32),
            jax.ShapeDtypeStruct((r // SEQ, d), F32),
        ],
        in_specs=[ANY, ANY, ANY, WHOLE, WHOLE, ANY, ANY, ANY, ANY, ANY, WHOLE, SCALARS, WHOLE, WHOLE],
        out_specs=[ANY, WHOLE, WHOLE, WHOLE],
        scratch_shapes=[
            pltpu.VMEM((m, d), LOW),
            pltpu.VMEM((3, d, width), LOW),
            pltpu.VMEM((width, d), LOW),
            pltpu.VMEM((m, 3 * width), LOW),
            pltpu.VMEM((m, width), LOW),
            pltpu.VMEM((m, d), LOW),
            pltpu.VMEM((m, 3 * width), LOW),
            pltpu.VMEM((rb, width), LOW),
            pltpu.VMEM((r, d), F32),
            pltpu.VMEM((r, d), F32),
            pltpu.VMEM((2, 4 * real, tile), LOW),
            sems(7),
            sems(2, 1),
            *Gather.scratch(chips, blocks),
            *Scatter.scratch(chips, blocks, r, d),
        ],
        compiler_params=params(3),
        name="attn_bwd",
    )(x, rows, before, picked, gain, qkv, mixed, normed, wqkv, wout, selector, starts, *tables)


def weight_grad(a, b, plane, inner):
    m, wide = a.shape
    n = b.shape[-1]
    nb = 256 if n % 256 == 0 else 128
    share = wide // inner

    def kernel(x, y, *refs):
        outs, total = refs[:-1], refs[-1]
        side = lax.rem(lax.axis_index("dp"), inner)
        total[...] = dot(x[...], y[...], 0, 0).astype(LOW)
        for j, out in enumerate(outs):
            at = pl.multiple_of(lax.rem(side + j, inner) * share, share)
            out[...] = total[pl.ds(at, share)]

    return pl.pallas_call(
        kernel,
        grid=(n // nb,),
        out_shape=[jax.ShapeDtypeStruct((share, n), LOW)] * inner,
        in_specs=[resident((m, wide)), pl.BlockSpec((None, m, nb), lambda i: (plane, 0, i))],
        out_specs=[pl.BlockSpec((share, nb), lambda i: (0, i))] * inner,
        scratch_shapes=[pltpu.VMEM((wide, nb), LOW)],
        compiler_params=params(),
        cost_estimate=pl.CostEstimate(
            flops=2 * m * wide * n, bytes_accessed=2 * (m * (wide + n) + wide * n), transcendentals=0
        ),
        name="weight_grad",
    )(a, b)


OUTER = 4
CHUNK = 80


def sum_kernel(inner, group, early, halves, late_pieces, *refs):
    count = len(halves)
    full, refs = refs[:count], refs[count:]
    got, refs = refs[:early], refs[early:]
    small, out, small_out, refs = *refs[:3], refs[3:]
    loc, rc, rb1, rb2, tot, refs = *refs[:5], refs[5:]
    load, late_send, late_recv, s1, r1, s2, r2, s3, r3, s4, r4, keep, refs = *refs[:12], refs[12:]
    sm0, sm1, sm2, small_send, small_recv = refs
    dp = lax.axis_index("dp")
    mp = lax.axis_index("mp")
    place, side = dp // inner, lax.rem(dp, inner)
    outside = jnp.logical_or(place == 0, place == OUTER - 1)
    inside = jnp.logical_not(outside)
    beside = jnp.where(place < OUTER // 2, 1 - place, 5 - place)
    across = (OUTER - 1) - place
    peers = [lax.rem(side + j, inner) for j in range(1, inner)]
    at = lambda p, i: (p * inner + i, mp)

    rounds = []
    me = (mp, side, place)
    others = [
        [(dp, lax.rem(mp + j, group)) for j in range(1, group)],
        [at(place, peer) for peer in peers],
        [at(lax.rem(place + j, OUTER), side) for j in range(1, OUTER)],
    ]
    used = 0
    for mine, buf, devices in zip(me, (sm0, sm1, sm2), others):
        copies = []
        for device in devices:
            copies.append(
                pltpu.make_async_remote_copy(
                    src_ref=buf.at[mine], dst_ref=buf.at[mine], send_sem=small_send.at[used],
                    recv_sem=small_recv.at[used], device_id=device, device_id_type=MESH,
                )
            )
            used += 1
        rounds.append((mine, buf, copies))

    def small_round(i):
        if i:
            for copy in rounds[i - 1][2]:
                copy.wait()
            buf = rounds[i - 1][1]
            value = buf[0]
            for j in range(1, buf.shape[0]):
                value += buf[j]
        else:
            value = small[...]
        if i < len(rounds):
            mine, buf, copies = rounds[i]
            buf[mine] = value
            for copy in copies:
                copy.start()
        else:
            small_out[...] = value

    barrier = pltpu.get_barrier_semaphore()
    for devices in others:
        for device in devices:
            pl.semaphore_signal(barrier, inc=1, device_id=device, device_id_type=MESH)
    pl.semaphore_wait(barrier, sum(len(devices) for devices in others))

    offsets = [sum(halves[:p]) for p in range(count)]
    chunks = sum(halves) // CHUNK

    late = count - 1
    late_copies = []
    for j, peer in enumerate(peers):
        for c in range(late_pieces):
            rows = halves[late] // late_pieces
            late_copies.append(
                pltpu.make_async_remote_copy(
                    src_ref=full[late].at[pl.ds(peer * halves[late] + c * rows, rows)],
                    dst_ref=rc.at[j, pl.ds(offsets[late] + c * rows, rows)],
                    send_sem=late_send.at[j * late_pieces + c],
                    recv_sem=late_recv.at[j * late_pieces + c],
                    device_id=at(place, peer),
                    device_id_type=MESH,
                )
            )
    for copy in late_copies:
        copy.start()

    loads = []
    for p in range(count):
        own = full[p] if p < early else full[p].at[pl.ds(side * halves[p], halves[p])]
        one = [(own, loc.at[pl.ds(offsets[p], halves[p])])]
        if p < early:
            for j in range(inner - 1):
                one.append((got[p].at[j], rc.at[j, pl.ds(offsets[p], halves[p])]))
        loads.append(
            [pltpu.make_async_copy(a, b, load.at[p * inner + i]) for i, (a, b) in enumerate(one)]
        )
    for one in loads:
        for copy in one:
            copy.start()
    small_round(0)

    def to_beside(src, dst, send, recv, t):
        rows = pl.ds(t * CHUNK, CHUNK)
        return pltpu.make_async_remote_copy(
            src_ref=src.at[rows], dst_ref=dst.at[rows], send_sem=send.at[t], recv_sem=recv.at[t],
            device_id=at(beside, side), device_id_type=MESH,
        )

    def to_across(t):
        rows = pl.ds(t * CHUNK, CHUNK)
        return pltpu.make_async_remote_copy(
            src_ref=loc.at[rows], dst_ref=rb2.at[rows], send_sem=s2.at[t], recv_sem=r2.at[t],
            device_id=at(across, side), device_id_type=MESH,
        )

    def to_peer(j, t):
        rows = pl.ds(t * CHUNK, CHUNK)
        return pltpu.make_async_remote_copy(
            src_ref=tot.at[rows], dst_ref=out.at[side, rows], send_sem=s4.at[j, t], recv_sem=r4.at[j, t],
            device_id=at(place, peers[j]), device_id_type=MESH,
        )

    def to_self(t):
        rows = pl.ds(t * CHUNK, CHUNK)
        return pltpu.make_async_copy(tot.at[rows], out.at[side, rows], keep.at[t])

    def hand_out(t):
        for j in range(inner - 1):
            to_peer(j, t).start()
        to_self(t).start()

    def step(t, carry):
        rows = pl.ds(pl.multiple_of(t * CHUNK, CHUNK), CHUNK)

        for i in range(1, len(rounds) + 1):

            @pl.when(t == 2 * i)
            def _(i=i):
                small_round(i)

        @pl.when(t < chunks)
        def _():
            for p in range(count):

                @pl.when(t == offsets[p] // CHUNK)
                def _(p=p):
                    for copy in loads[p]:
                        copy.wait()

            for c in range(late_pieces):

                @pl.when(t == (offsets[late] + c * (halves[late] // late_pieces)) // CHUNK)
                def _(c=c):
                    for j in range(inner - 1):
                        late_copies[j * late_pieces + c].wait_recv()

            total = loc[rows].astype(F32)
            for j in range(inner - 1):
                total += rc[j, rows].astype(F32)
            loc[rows] = total.astype(LOW)

            @pl.when(outside)
            def _():
                to_beside(loc, rb1, s1, r1, t).start()

            @pl.when(inside)
            def _():
                to_beside(loc, rb1, s1, r1, t).wait_recv()
                loc[rows] = (loc[rows].astype(F32) + rb1[rows].astype(F32)).astype(LOW)
                to_across(t).start()

        u = t - 1

        @pl.when(jnp.logical_and(inside, jnp.logical_and(u >= 0, u < chunks)))
        def _():
            ready = pl.ds(pl.multiple_of(u * CHUNK, CHUNK), CHUNK)
            to_across(u).wait_recv()
            tot[ready] = (loc[ready].astype(F32) + rb2[ready].astype(F32)).astype(LOW)
            to_beside(tot, tot, s3, r3, u).start()
            hand_out(u)

        w = t - LAG

        @pl.when(jnp.logical_and(outside, w >= 0))
        def _():
            to_beside(tot, tot, s3, r3, w).wait_recv()
            hand_out(w)

        return carry

    lax.fori_loop(0, chunks + LAG, step, 0)

    def finish(t, carry):
        @pl.when(outside)
        def _():
            to_beside(loc, rb1, s1, r1, t).wait_send()

        @pl.when(inside)
        def _():
            to_across(t).wait_send()
            to_beside(tot, tot, s3, r3, t).wait_send()

        for j in range(inner - 1):
            to_peer(j, t).wait()
        to_self(t).wait()
        return carry

    lax.fori_loop(0, chunks, finish, 0)
    for copy in late_copies:
        copy.wait_send()


LAG = 6


class Reducer:
    def __init__(self, mesh):
        self.inner = mesh.shape["dp"] // OUTER
        self.group = mesh.shape["mp"]

    def exchange(self, shares):
        got = []
        for j in range(1, self.inner):
            pairs = []
            for o in range(OUTER):
                for i in range(self.inner):
                    pairs.append((o * self.inner + i, o * self.inner + (i + j) % self.inner))
            got.append(lax.ppermute(shares[j], "dp", pairs)[None])
        return got[0] if len(got) == 1 else jnp.concatenate(got, 0)

    def reduce(self, own, got, last, small):
        inner = self.inner
        width = last.shape[1]
        pieces = [*own, last]
        halves = tuple(p.shape[0] for p in own) + (last.shape[0] // inner,)
        share = sum(halves)
        chunks = share // CHUNK
        any_spec = pl.BlockSpec(memory_space=pl.ANY)
        late_pieces = halves[-1] // CHUNK // 2
        buffer = pltpu.VMEM((share, width), LOW)
        return pl.pallas_call(
            functools.partial(sum_kernel, inner, self.group, len(got), halves, late_pieces),
            out_shape=[
                jax.ShapeDtypeStruct((inner, share, width), LOW),
                jax.ShapeDtypeStruct(small.shape, F32),
            ],
            in_specs=[any_spec] * (len(pieces) + len(got)) + [pl.BlockSpec(memory_space=pltpu.VMEM)],
            out_specs=[any_spec, pl.BlockSpec(memory_space=pltpu.VMEM)],
            scratch_shapes=[
                buffer,
                pltpu.VMEM((inner - 1, share, width), LOW),
                buffer,
                buffer,
                buffer,
                sems(len(pieces) * inner),
                sems((inner - 1) * late_pieces),
                sems((inner - 1) * late_pieces),
                *[sems(chunks) for _ in range(6)],
                sems(inner - 1, chunks),
                sems(inner - 1, chunks),
                sems(chunks),
                pltpu.VMEM((self.group, *small.shape), F32),
                pltpu.VMEM((inner, *small.shape), F32),
                pltpu.VMEM((OUTER, *small.shape), F32),
                sems(self.group + inner + OUTER - 3),
                sems(self.group + inner + OUTER - 3),
            ],
            compiler_params=pltpu.CompilerParams(
                collective_id=0, has_side_effects=True, vmem_limit_bytes=VMEM_LIMIT
            ),
            cost_estimate=pl.CostEstimate(flops=0, bytes_accessed=600_000_000, transcendentals=0),
            name="sum_over_dp",
        )(*pieces, *got, small)


def body(
    mesh,
    rows,
    lengths,
    freq_class,
    freq_table,
    gain_attn,
    gain_mlp,
    w_qkv,
    w_out,
    w_gate_up,
    w_down,
    cotangent,
):
    reducer = Reducer(mesh)
    group_size = mesh.shape["mp"]
    chips = group_size // 2
    local_rows, d = rows.shape
    own_series = local_rows // SEQ
    mp_index = lax.axis_index("mp")
    heads_width = w_out.shape[0]
    head_count = heads_width // HS
    ff = w_down.shape[0]

    places = jnp.arange(group_size, dtype=jnp.int32)
    owners = ((mp_index // 2 + places // 2) % chips) * 2 + (mp_index % 2 + places) % 2
    starts = (SEQ - lengths.reshape(group_size, own_series))[owners]
    tables = slot_tables()
    slots = jnp.arange(SEQ, dtype=jnp.int32)
    mine_valid = (slots[None, :] >= starts[0][:, None]).astype(F32)
    starts = starts.reshape(-1)

    by_class = [(freq_class == f)[:, None] for f in range(NFREQ)]
    picked = freq_table[NFREQ - 1][None]
    for f in range(NFREQ - 1):
        picked = jnp.where(by_class[f], freq_table[f][None], picked)
    selector = head_selector(head_count)

    qkv, mixed, normed, qkv_low, out_low, gate_low, down_low, after_attn, normed_mlp, grad_low = attn_forward(
        chips, rows, cotangent, picked, gain_attn[None], gain_mlp[None], w_qkv, w_out, w_gate_up, w_down, selector,
        starts, tables,
    )
    grad_pre, normed_mlp, down_own, down_far, *rest = mlp_both(
        chips, reducer.inner, normed_mlp, grad_low, after_attn, cotangent, gain_mlp[None], gate_low, down_low, starts
    )
    shares, (grad_after, grad_after_low, gains_mlp) = [rest[: reducer.inner]], rest[reducer.inner :]
    ups = [weight_grad(normed_mlp, grad_pre, c, reducer.inner) for c in range(2)]
    if ff >= d:
        shares += ups
    else:
        shares.append([jnp.concatenate(both, 1) for both in zip(*ups)])
    got = [reducer.exchange(v) for v in shares]
    output = after_attn + down_own.astype(F32)
    for k in range(1, chips):
        far = lax.ppermute(down_far[k - 1], "mp", [(i, (i + 2 * k) % group_size) for i in range(group_size)])
        output += far.astype(F32)

    last, grad_rows, gains_attn, series_sums = attn_backward(
        chips, grad_after_low, rows, grad_after, picked, gain_attn[None], qkv, mixed, normed, qkv_low, out_low,
        selector, starts, tables,
    )
    grad_table = [jnp.sum(jnp.where(by_class[f], series_sums, 0.0), 0) for f in range(NFREQ)]

    tokens = jnp.full((d,), jnp.sum(mine_valid))
    zero = jnp.zeros((d,), F32)
    small = jnp.stack([gains_attn[0], gains_mlp[0], *grad_table, tokens, zero, zero])
    own = [v[0] for v in shares]
    sums, small = reducer.reduce(own, got, last, small)
    root_scale = lax.rsqrt(small[2 + NFREQ, 0])
    small = small * root_scale
    finals, offset = [], 0
    for share in [v.shape[0] for v in own] + [last.shape[0] // reducer.inner]:
        finals.append(sums[:, offset : offset + share].reshape(-1, d))
        offset += share
    down_out = finals[0].astype(F32) * root_scale
    if len(finals) == 3:
        gate_up_out = jnp.stack([finals[1][:, :ff], finals[1][:, ff:]]).astype(F32) * root_scale
    else:
        gate_up_out = jnp.stack(finals[1:3]).astype(F32) * root_scale
    identity = jnp.eye(heads_width, dtype=LOW)
    last = finals[-1]
    qkv_out = jnp.stack(
        [dot(last[c * heads_width : (c + 1) * heads_width], identity, 0, 0) * root_scale for c in range(3)]
    )
    out_out = last[3 * heads_width :].astype(F32) * root_scale
    return (
        output,
        grad_rows,
        qkv_out,
        out_out,
        gate_up_out,
        down_out,
        small[0],
        small[1],
        small[2 : 2 + NFREQ],
    )


def solution(mesh):
    return jax.shard_map(
        functools.partial(body, mesh),
        mesh=mesh,
        in_specs=(
            P(("dp", "mp"), None),
            P("dp"),
            P(("dp", "mp")),
            P(),
            P(),
            P(),
            P(None, None, "mp"),
            P("mp", None),
            P(None, None, "mp"),
            P("mp", None),
            P(("dp", "mp"), None),
        ),
        out_specs=(
            P(("dp", "mp"), None),
            P(("dp", "mp"), None),
            P(None, None, "mp"),
            P("mp", None),
            P(None, None, "mp"),
            P("mp", None),
            P(),
            P(),
            P(),
        ),
        check_vma=False,
    )
```
